32 devices in a mesh: section: 2 (over core), dp: 16 (over z, y, x).
Axes of the slice: x: 2, y: 2, z: 4, core: 2. Of those that a mesh axis runs over, the one named last changes fastest.
Arguments:
- layer_input: bfloat16 [4096, 1024], P(('section', 'dp')), may hold values from -6 to 6
- skip_input: bfloat16 [4096, 1024], P(('section', 'dp')), may hold values from -6 to 6
- segment_ids: int32 [16, 2, 128], P('dp'), may hold values from 0 to 3, never falling along the last dimension, each value on 1 to 96 neighbouring positions
- out_cotangent: bfloat16 [4096, 1024], P(('section', 'dp')), may hold values from -6 to 6
- merger: bfloat16 [2048, 1024], P('section'), may hold values from -0.125 to 0.125
- mixing: bfloat16 [1024, 3072], P('section'), may hold values from -0.1875 to 0.1875
- readout: bfloat16 [1024, 1024], P('section'), may hold values from -0.75 to 0.75
- expand: bfloat16 [1024, 4096], P('section'), may hold values from -0.1875 to 0.1875
- narrow: bfloat16 [4096, 1024], P('section'), may hold values from -0.09375 to 0.09375
- first_gain: bfloat16 [1024], P('section'), may hold values from 0.5 to 1.5
- first_bias: bfloat16 [1024], P('section'), may hold values from -1.5 to 1.5
- second_gain: bfloat16 [1024], P('section'), may hold values from 0.5 to 1.5
- second_bias: bfloat16 [1024], P('section'), may hold values from -1.5 to 1.5
- up_bias: bfloat16 [4096], P('section'), may hold values from -2.5 to 2.5
Outputs:
- block_output: bfloat16 [4096, 1024], P(('section', 'dp'))
- input_grad: bfloat16 [4096, 1024], P(('section', 'dp'))
- skip_grad: bfloat16 [4096, 1024], P(('section', 'dp'))
- merger_grad: float32 [2048, 1024], P('section', 'dp')
- mixing_grad: float32 [1024, 3072], P('section', 'dp')
- readout_grad: float32 [1024, 1024], P('section', 'dp')
- expand_grad: float32 [1024, 4096], P('section', 'dp')
- narrow_grad: float32 [4096, 1024], P('section', 'dp')
- first_gain_grad: float32 [1024], P('section')
- first_bias_grad: float32 [1024], P('section')
- second_gain_grad: float32 [1024], P('section')
- second_bias_grad: float32 [1024], P('section')
- up_bias_grad: float32 [4096], P('section')
The draws below stay inside these ranges and needn't reach their ends.
Inputs may be any that keep to these rules, and one draw needn't show every extreme that they name: `segment_ids`: each row of 128 frames holds 4 utterances one after another, numbered from 0 and never falling, each 1 to 96 frames long; one row's utterances never continue in another row.
All inputs are finite; a program needn't handle non-finite values.
Results may differ from the reference program's by a relative error of at most 0.015.
Values may be sent and summed in bfloat16 or wider, within the bound.
No kernel may reach another device: no remote copies, remote signals or barrier semaphores. Data moves between devices by JAX's collectives and lax.ppermute only.
A program may use at most 192 MiB of HBM per device.

```python
import math
import jax
import jax.numpy as jnp
import numpy as np
from jax import lax

D = 1024
HEADS = 16
HEAD_DIM = 64
FF = 4096
TOK_DEV = 128
SEGS = 4
MOST = 96
TOKENS = 4096
N_DP = 16


def spiked(result, stream_key, source, target, parts, factor):
    owner, partner = [(jnp.arange(result.shape[position]) // (result.shape[position] // parts)).reshape([-1 if axis == position else 1 for axis in range(result.ndim)]) for position in (source, target)]
    chosen = jax.random.permutation(stream_key, parts)[partner]
    strong = (owner == chosen) | (owner == (partner + parts // 2) % parts)
    return jnp.where(strong, factor * result, result)


def steps_of(own_key, shape, cuts, smallest, largest):
    level, own = 1.0, jax.random.fold_in(own_key, 6)
    for axis_at, parts in cuts:
        draws = jnp.exp(jax.random.uniform(jax.random.fold_in(own, axis_at), (parts,), jnp.float32, smallest / len(cuts), largest / len(cuts)))
        level = level * jnp.repeat(draws, shape[axis_at] // parts).reshape([-1 if axis == axis_at else 1 for axis in range(len(shape))])
    return level


def split_up(number_of, total, limit, slope):
    portions = [(1 << 20) // math.isqrt(standing ** slope) + 1 for standing in range(2, number_of + 1)]
    spare, counts = total - limit - (number_of - 1), [1] * (number_of - 1)
    while spare > 0:
        candidates = [i for i in range(number_of - 1) if counts[i] < limit]
        pool, left = sum([portions[i] for i in candidates]), spare
        for i in candidates:
            more = min(limit - counts[i], max(1, left * portions[i] // pool), spare)
            counts[i] = counts[i] + more
            spare = spare - more
    return np.array([limit] + counts)


def uneven_parts(key, amount, total, reach, slope):
    if amount == 2:
        one = jax.random.randint(key, (), max(1, total - reach), min(reach, total - 1) + 1)
        return jnp.stack([one, total - one])
    lengths = jnp.asarray(split_up(amount, total, reach, slope), jnp.int32)
    twos = (amount - 1) // 2
    source_of, sink = lengths[1:1 + 2 * twos:2], lengths[2:2 + 2 * twos:2]
    room = jnp.minimum(source_of - 1, reach - sink)
    shifted = jax.random.randint(jax.random.fold_in(key, 1), (twos,), 0, 1 << 20) % (room + 1)
    lengths = lengths.at[1:1 + 2 * twos:2].set(source_of - shifted).at[2:2 + 2 * twos:2].set(sink + shifted)
    return lengths[jax.random.permutation(jax.random.fold_in(key, 2), amount)]


def centred(stream_key, dims, scale, reach, shards=(), kind=jnp.bfloat16):
    values = scale * jax.random.normal(stream_key, dims, jnp.float32)
    if shards:
        values = values * steps_of(stream_key, dims, shards, -0.22, 0.18)
    return jnp.clip(values, -reach, reach).astype(kind)


def heavy_noise(own_key, dims, scale, most, pieces, heavy, kind=jnp.bfloat16):
    entries = scale * jax.random.normal(own_key, dims, jnp.float32)
    if pieces:
        entries = entries * steps_of(own_key, dims, pieces, -0.22, 0.18)
    return jnp.clip(spiked(entries, jax.random.fold_in(own_key, 3), *heavy), -most, most).astype(kind)


def setup_inputs(seed: int = 0) -> dict:
    seeds = jax.random.split(jax.random.key(seed), 15)
    return {
        "layer_input": centred(seeds[0], (TOKENS, D), 1.0, 6.0, ((0, 32),)),
        "skip_input": centred(seeds[1], (TOKENS, D), 1.0, 6.0, ((0, 32),)),
        "segment_ids": jax.vmap(lambda own: jnp.searchsorted(jnp.cumsum(uneven_parts(own, SEGS, TOK_DEV, MOST, 2)), jnp.arange(TOK_DEV), side="right"))(jax.random.split(seeds[2], N_DP * 2)).reshape((N_DP, 2, TOK_DEV)).astype(jnp.int32),
        "out_cotangent": heavy_noise(seeds[3], (TOKENS, D), 1.0, 6.0, ((0, 32),), (0, 1, 32, 2.75)),
        "merger": centred(seeds[4], (2 * D, D), (2 * D) ** -0.5, 0.125, ((0, 2),)),
        "mixing": centred(seeds[5], (D, 3 * D), D ** -0.5, 0.1875, ((0, 2),)),
        "readout": centred(seeds[6], (D, D), (D // 16) ** -0.5, 0.75, ((0, 2),)),
        "expand": centred(seeds[7], (D, FF), D ** -0.5, 0.1875, ((0, 2),)),
        "narrow": centred(seeds[8], (FF, D), FF ** -0.5, 0.09375, ((0, 2),)),
        "first_gain": jnp.clip(1.0 + 0.1 * jax.random.normal(seeds[9], (D,), jnp.float32), 0.5, 1.5).astype(jnp.bfloat16),
        "first_bias": centred(seeds[10], (D,), 0.3, 1.5, ((0, 2),)),
        "second_gain": jnp.clip(1.0 + 0.1 * jax.random.normal(seeds[11], (D,), jnp.float32), 0.5, 1.5).astype(jnp.bfloat16),
        "second_bias": centred(seeds[12], (D,), 0.3, 1.5, ((0, 2),)),
        "up_bias": centred(seeds[13], (FF,), 0.5, 2.5, ((0, 2),)),
    }


@jax.custom_vjp
def low(v):
    return lax.optimization_barrier(v.astype(jnp.bfloat16)).astype(jnp.float32)

@jax.custom_vjp
def low_back(v):
    return v

def low_keep(v):
    return (low(v), None)

def low_pass(kept, grad):
    return (grad,)

def back_keep(v):
    return (v, None)

def back_low(kept, grad):
    return (low(grad),)
low.defvjp(low_keep, low_pass)
low_back.defvjp(back_keep, back_low)

def hdot(left, right):
    return jnp.dot(left, right, precision=lax.Precision.HIGHEST, preferred_element_type=jnp.float32)

def layer_norm(values, gain, offset):
    center = values - lax.optimization_barrier(jnp.mean(values, -1, keepdims=True))
    spread = lax.optimization_barrier(jnp.mean(center * center, -1, keepdims=True))
    return center * lax.rsqrt(spread + 1e-05) * gain + offset

def alibi_bias(heads, length):
    places = jnp.arange(length).astype(jnp.float32)
    apart = jnp.abs(places[:, None] - places[None, :])
    slopes = jnp.exp2(-8.0 * (jnp.arange(heads).astype(jnp.float32) + 1.0) / heads)
    return -slopes[:, None, None] * apart[None]

def attend_block(packed):
    mixed_block, segments = packed
    queries = mixed_block[:, 0]
    key_rows = mixed_block[:, 1]
    value_rows = mixed_block[:, 2]
    raw = jnp.einsum('ihd,jhd->hij', queries, key_rows, precision=lax.Precision.HIGHEST) * 0.125
    raw = low_back(raw + alibi_bias(HEADS, TOK_DEV))
    same = segments[:, None] == segments[None, :]
    scores = jnp.where(same[None], raw, -1000000000.0)
    probs = jax.nn.softmax(scores, axis=-1)
    attended = jnp.einsum('hij,jhd->ihd', low(probs), value_rows, precision=lax.Precision.HIGHEST)
    return attended.reshape(TOK_DEV, D)

def forward(frames, merger, mixing, readout, expand, narrow, first_gain, first_bias, second_gain, second_bias, up_bias, segments):
    merged = low_back(hdot(frames, merger))
    first_norm = low(layer_norm(merged, first_gain, first_bias))
    mixed = low(low_back(hdot(first_norm, mixing)))
    blocks = mixed.reshape(TOKENS // TOK_DEV, TOK_DEV, 3, HEADS, HEAD_DIM)
    attended = lax.map(jax.checkpoint(attend_block), (blocks, segments)).reshape(TOKENS, D)
    attended = low(low_back(attended))
    residual = merged + low_back(hdot(attended, readout))
    second_norm = low(layer_norm(residual, second_gain, second_bias))
    lifted = low_back(hdot(second_norm, expand) + up_bias)
    activated = low(jax.nn.gelu(lifted, approximate=True))
    return residual + low_back(hdot(activated, narrow))

def reference(layer_input, skip_input, segment_ids, out_cotangent, merger, mixing, readout, expand, narrow, first_gain, first_bias, second_gain, second_bias, up_bias):
    frames = jnp.concatenate([layer_input.astype(jnp.float32), skip_input.astype(jnp.float32)], axis=1)
    segments = jnp.transpose(segment_ids, (1, 0, 2)).reshape(TOKENS // TOK_DEV, TOK_DEV)
    params = [w.astype(jnp.float32) for w in (merger, mixing, readout, expand, narrow, first_gain, first_bias, second_gain, second_bias, up_bias)]
    top = jnp.roll(out_cotangent.astype(jnp.float32), TOKENS // 2, axis=0)

    def wrapped(*inputs):
        return forward(*inputs, segments)
    output, backward = jax.vjp(wrapped, frames, *params)
    grads = backward(top)
    block_output = jnp.roll(output, TOKENS // 2, axis=0).astype(jnp.bfloat16)
    frame_grad = grads[0]
    return (block_output, frame_grad[:, :D].astype(jnp.bfloat16), frame_grad[:, D:].astype(jnp.bfloat16), grads[1], grads[2], grads[3], grads[4], grads[5], grads[6], grads[7], grads[8], grads[9], grads[10])
```

```python
from functools import partial

import jax
import jax.numpy as jnp
from jax import lax
from jax.sharding import PartitionSpec as P

HEAD_DIM = 64
LOW = jnp.bfloat16
FULL = jnp.float32


def torus_of(count):
    power = count.bit_length() - 1
    side = 1 << (power // 3)
    return {"x": side, "y": side, "z": count // (side * side)}


class Torus:
    def __init__(self, count):
        self.count = count
        self.sizes = torus_of(count)
        self.strides = {"x": 1, "y": self.sizes["x"], "z": self.sizes["x"] * self.sizes["y"]}

    def place(self, axis):
        return (lax.axis_index("dp") // self.strides[axis]) % self.sizes[axis]

    def shift(self, value, axis, step):
        size, stride = self.sizes[axis], self.strides[axis]
        pairs = []
        for source in range(self.count):
            spot = (source // stride) % size
            if 0 <= spot + step < size:
                pairs.append((source, source + step * stride))
        return lax.ppermute(value, "dp", pairs)

    def flip(self, value, mask):
        return lax.ppermute(value, "dp", [(source, source ^ mask) for source in range(self.count)])


def pair(value):
    return lax.ppermute(value, "section", [(0, 1), (1, 0)])


def layer_norm(values, gain, offset):
    center = values - jnp.mean(values, -1, keepdims=True)
    spread = jnp.mean(center * center, -1, keepdims=True)
    return center * lax.rsqrt(spread + 1e-05) * gain + offset


def alibi_bias(heads, length):
    places = jnp.arange(length).astype(FULL)
    apart = jnp.abs(places[:, None] - places[None, :])
    slopes = jnp.exp2(-8.0 * (jnp.arange(heads).astype(FULL) + 1.0) / heads)
    return -slopes[:, None, None] * apart[None]


def dot(left, right):
    return jnp.dot(left, right, preferred_element_type=FULL)


def contract_first(left, right):
    return lax.dot_general(left, right, (((0,), (0,)), ((), ())), preferred_element_type=FULL)


def contract_last(left, right):
    return lax.dot_general(left, right, (((1,), (1,)), ((), ())), preferred_element_type=FULL)


def scores_of(queries, key_rows, segments):
    raw = jnp.einsum("ihd,jhd->hij", queries, key_rows, preferred_element_type=FULL) * 0.125
    raw = raw + alibi_bias(queries.shape[1], queries.shape[0])
    same = segments[:, None] == segments[None, :]
    return jnp.where(same[None], raw, -1000000000.0)


def reduce_grad(torus, order, left, right):
    sizes = torus.sizes
    tokens, columns = right.shape
    block = columns // torus.count
    split = right.reshape(tokens, sizes["z"], sizes["y"], sizes["x"], block)
    names = ("z", "y", "x")
    split = split.transpose(*(1 + names.index(axis) for axis in order), 0, 4)
    first, rest = order[0], order[1:]

    def product(piece):
        lead = piece.shape[:-2]
        flat = piece.reshape(-1, tokens, block).transpose(1, 0, 2).reshape(tokens, -1)
        return contract_first(flat, left).reshape(*lead, block, left.shape[1])

    def stage(axis, take):
        size, here = sizes[axis], torus.place(axis)
        if size == 2:
            sent = torus.flip(take(1 - here).astype(LOW), torus.strides[axis])
            return take(here) + sent.astype(FULL)
        up = down = None
        for step in range(1, size):
            over = jnp.clip(here + size - step, 0, size - 1)
            under = jnp.clip(here - size + step, 0, size - 1)
            up_sum, down_sum = take(over), take(under)
            if up is not None:
                up_sum, down_sum = up_sum + up, down_sum + down
            up = torus.shift(up_sum.astype(LOW), axis, 1).astype(FULL)
            down = torus.shift(down_sum.astype(LOW), axis, -1).astype(FULL)
        own = take(here)
        return own if up is None else own + up + down

    total = stage(first, lambda spot: product(lax.dynamic_index_in_dim(split, spot, 0, False)))
    for axis in rest:
        held = total.astype(LOW)
        total = stage(
            axis, lambda spot: lax.dynamic_index_in_dim(held, spot, 0, False).astype(FULL)
        )
    return total


def body(
    layer_input,
    skip_input,
    segment_ids,
    out_cotangent,
    merger,
    mixing,
    readout,
    expand,
    narrow,
    first_gain,
    first_bias,
    second_gain,
    second_bias,
    up_bias,
):
    torus = Torus(lax.axis_size("dp"))
    section = lax.axis_index("section")
    rows, width = layer_input.shape
    heads = width // HEAD_DIM
    first_core = section == 0

    def mine(value):
        half = value.shape[1] // 2
        return lax.dynamic_slice_in_dim(value, section * half, half, 1)

    def other(value):
        half = value.shape[1] // 2
        return lax.dynamic_slice_in_dim(value, (1 - section) * half, half, 1)

    def joined(own, far, axis):
        return jnp.where(
            first_core,
            jnp.concatenate([own, far], axis=axis),
            jnp.concatenate([far, own], axis=axis),
        )

    merger_far = pair(merger)
    vectors = jnp.concatenate([first_gain, first_bias, second_gain, second_bias, up_bias])
    vectors_far = pair(vectors)
    mixing_far = pair(mixing)
    readout_far = pair(readout)
    expand_far = pair(expand)
    narrow_far = pair(narrow)
    top_low = pair(out_cotangent)

    bounds = []
    start = 0
    for part in (first_gain, first_bias, second_gain, second_bias, up_bias):
        bounds.append((start, start + part.shape[0]))
        start += part.shape[0]
    gain_one, bias_one, gain_two, bias_two, bias_up = (
        joined(vectors[low:high], vectors_far[low:high], 0).astype(FULL) for low, high in bounds
    )

    def apply(value, near, far):
        return dot(mine(value), near) + dot(other(value), far)

    def pull(grad, near, far):
        return joined(contract_last(grad, near), contract_last(grad, far), 1)

    frames_mine = jnp.where(first_core, layer_input, skip_input)
    frames_other = jnp.where(first_core, skip_input, layer_input)
    merged = dot(frames_mine, merger) + dot(frames_other, merger_far)
    first_norm, first_back = jax.vjp(layer_norm, merged, gain_one, bias_one)
    first_low = first_norm.astype(LOW)
    mixed = apply(first_low, mixing, mixing_far).astype(LOW)
    mixed = mixed.reshape(rows, 3, heads, HEAD_DIM)
    queries, key_rows, value_rows = mixed[:, 0], mixed[:, 1], mixed[:, 2]
    segments = lax.dynamic_index_in_dim(segment_ids[0], section, 0, keepdims=False)
    scores = scores_of(queries, key_rows, segments)
    log_total = jax.nn.logsumexp(scores, axis=-1, keepdims=True)
    probs = jnp.exp(scores - log_total)
    probs_low = probs.astype(LOW)
    attended = jnp.einsum("hij,jhd->ihd", probs_low, value_rows, preferred_element_type=FULL)
    attended = attended.reshape(rows, width).astype(LOW)
    residual = merged + apply(attended, readout, readout_far)
    second_norm, second_back = jax.vjp(layer_norm, residual, gain_two, bias_two)
    second_low = second_norm.astype(LOW)
    lifted = apply(second_low, expand, expand_far) + bias_up
    activated, gelu_back = jax.vjp(partial(jax.nn.gelu, approximate=True), lifted)
    activated_low = activated.astype(LOW)
    output = residual + apply(activated_low, narrow, narrow_far)
    block_output = pair(output.astype(LOW))

    def both(value):
        return jnp.concatenate([value, pair(value)], axis=0)

    def halves(value):
        return jnp.concatenate([mine(value), pair(other(value))], axis=0)

    def grad_of(order, left, right):
        return reduce_grad(torus, order, left, right)

    tops = both(top_low)
    narrow_grad = grad_of("xyz", halves(activated_low), tops)
    activated_grad = pull(top_low, narrow, narrow_far)
    (lifted_grad,) = gelu_back(activated_grad)
    lifted_low = lifted_grad.astype(LOW)
    up_bias_grad = jnp.sum(lifted_low.astype(FULL), axis=0)
    expand_grad = grad_of("yxz", halves(second_low), both(lifted_low))
    second_grad = pull(lifted_low, expand, expand_far)
    residual_part, second_gain_grad, second_bias_grad = second_back(second_grad)
    residual_grad = top_low.astype(FULL) + residual_part
    residual_low = residual_grad.astype(LOW)
    readout_grad = grad_of("yxz", halves(attended), both(residual_low))
    attended_grad = pull(residual_low, readout, readout_far).astype(LOW)
    attended_grad = attended_grad.reshape(rows, heads, HEAD_DIM)
    prob_grad = jnp.einsum("ihd,jhd->hij", attended_grad, value_rows, preferred_element_type=FULL)
    value_grad = jnp.einsum("hij,ihd->jhd", probs_low, attended_grad, preferred_element_type=FULL)
    score_grad = probs * (prob_grad - jnp.sum(probs * prob_grad, -1, keepdims=True))
    score_low = score_grad.astype(LOW)
    query_grad = (
        jnp.einsum("hij,jhd->ihd", score_low, key_rows, preferred_element_type=FULL) * 0.125
    )
    key_grad = jnp.einsum("hij,ihd->jhd", score_low, queries, preferred_element_type=FULL) * 0.125
    mixed_grad = (
        jnp.stack([query_grad, key_grad, value_grad], axis=1).reshape(rows, 3 * width).astype(LOW)
    )
    mixing_grad = grad_of("xyz", halves(first_low), both(mixed_grad))
    first_grad = pull(mixed_grad, mixing, mixing_far)
    merged_part, first_gain_grad, first_bias_grad = first_back(first_grad)
    merged_low = (residual_grad + merged_part).astype(LOW)
    frames_left = jnp.concatenate([frames_mine, pair(frames_other)], axis=0)
    merger_grad = grad_of("yxz", frames_left, both(merged_low))
    near_grad = contract_last(merged_low, merger).astype(LOW)
    far_grad = contract_last(merged_low, merger_far).astype(LOW)
    input_grad = jnp.where(first_core, near_grad, far_grad)
    skip_grad = jnp.where(first_core, far_grad, near_grad)

    keep, give = [], []
    for part in (first_gain_grad, first_bias_grad, second_gain_grad, second_bias_grad, up_bias_grad):
        keep.append(mine(part[None])[0])
        give.append(other(part[None])[0])
    small = jnp.concatenate(keep) + pair(jnp.concatenate(give))
    small = small.reshape(-1, 128)
    mask = 1
    while mask < torus.count:
        small = small + torus.flip(small, mask)
        mask *= 2
    small = small.reshape(-1)
    matrices = tuple(
        grad.T for grad in (merger_grad, mixing_grad, readout_grad, expand_grad, narrow_grad)
    )
    return (block_output, input_grad, skip_grad) + matrices + tuple(
        small[low:high] for low, high in bounds
    )


def solution(mesh):
    tokens = P(("section", "dp"), None)
    matrix, vector = P("section", None), P("section")
    placed = (tokens, tokens, P("dp", None, None), tokens) + (matrix,) * 5 + (vector,) * 5
    made = (tokens,) * 3 + (P("section", "dp"),) * 5 + (vector,) * 5
    return jax.shard_map(body, mesh=mesh, in_specs=placed, out_specs=made, check_vma=False)
```

```python
import jax
import jax.numpy as jnp
from jax import lax
from jax.experimental import pallas as pl
from jax.experimental.pallas import tpu as pltpu
from jax.sharding import PartitionSpec as P

HEAD_DIM = 64
LOW = jnp.bfloat16
FULL = jnp.float32


class Torus:
    def __init__(self, count):
        power = count.bit_length() - 1
        side = power // 3
        self.count, self.power = count, power
        self.bits = {
            "x": list(range(side)),
            "y": list(range(side, 2 * side)),
            "z": list(range(2 * side, power)),
        }

    def order(self, axis):
        lead = self.bits[axis]
        across = self.bits["y" if axis == "x" else "x"]
        return lead[0], across + lead[1:] + self.bits["z"]

    def bit(self, bit):
        return (lax.axis_index("dp") >> bit) & 1

    def flip(self, value, bit):
        pairs = [(source, source ^ (1 << bit)) for source in range(self.count)]
        return lax.ppermute(value, "dp", pairs)


def pair(value):
    return lax.ppermute(value, "section", [(0, 1), (1, 0)])


def dot(left, right):
    return jnp.dot(left, right, preferred_element_type=FULL)


def contract_first(left, right):
    return lax.dot_general(left, right, (((0,), (0,)), ((), ())), preferred_element_type=FULL)


def contract_last(left, right):
    return lax.dot_general(left, right, (((1,), (1,)), ((), ())), preferred_element_type=FULL)


def nrm_stats(values):
    center = values - jnp.mean(values, -1, keepdims=True)
    scale = lax.rsqrt(jnp.mean(center * center, -1, keepdims=True) + 1e-05)
    return center * scale, scale


def nrm_back(xhat, scale, grad, gain):
    g = grad * gain
    inner = g - jnp.mean(g, -1, keepdims=True) - xhat * jnp.mean(g * xhat, -1, keepdims=True)
    return scale * inner


def part(ref, section, far):
    half = ref.shape[1] // 2
    spot = (1 - section) if far else section
    return ref.at[:, pl.ds(pl.multiple_of(spot * half, half), half)]


def merge_kernel(near_x, far_x, near_w, far_w, gain, bias, merged, low):
    total = dot(near_x[...], near_w[...]) + dot(far_x[...], far_w[...])
    merged[...] = total
    xhat, _ = nrm_stats(total)
    low[...] = (xhat * gain[...] + bias[...]).astype(LOW)


def score_parts(heads, seg_rows, seg_cols):
    rows = seg_rows.shape[0]
    same = seg_rows == seg_cols
    spots = [lax.broadcasted_iota(jnp.int32, (rows, rows), axis) for axis in (0, 1)]
    apart = jnp.abs(spots[0] - spots[1]).astype(FULL)
    slopes = [2.0 ** (-8.0 * (head + 1) / heads) for head in range(heads)]
    lane = lax.broadcasted_iota(jnp.int32, (rows, 2 * HEAD_DIM), 1)
    return same, apart, slopes, lane < HEAD_DIM


def probs_of(query, keys, slope, apart, same):
    raw = contract_last(query, keys) * 0.125 - slope * apart
    raw = jnp.where(same, raw, -1000000000.0)
    raised = jnp.exp(raw - jnp.max(raw, -1, keepdims=True))
    return raised / jnp.sum(raised, -1, keepdims=True)


def attend_kernel(
    where, low, merged, seg_rows, seg_cols, mix_near, mix_far, read_near, read_far, gain, bias,
    mixed, attended, residual, second,
):
    section = where[0]
    width = low.shape[1]
    heads = width // HEAD_DIM
    near, far = part(low, section, False)[...], part(low, section, True)[...]
    step = width // 2
    for base in range(0, 3 * width, step):
        block = dot(near, mix_near[:, base : base + step]) + dot(far, mix_far[:, base : base + step])
        mixed[:, base : base + step] = block.astype(LOW)
    same, apart, slopes, first = score_parts(heads, seg_rows[...], seg_cols[...])
    for two in range(heads // 2):
        lanes = slice(two * 128, two * 128 + 128)
        query = mixed[:, lanes]
        keys = mixed[:, width + two * 128 : width + two * 128 + 128]
        values = mixed[:, 2 * width + two * 128 : 2 * width + two * 128 + 128]
        blank = jnp.zeros_like(query)
        outs = []
        for head in (0, 1):
            own = jnp.where(first, query, blank) if head == 0 else jnp.where(first, blank, query)
            probs = probs_of(own, keys, slopes[2 * two + head], apart, same)
            outs.append(dot(probs.astype(LOW), values))
        attended[:, lanes] = jnp.where(first, outs[0], outs[1]).astype(LOW)
    total = merged[...] + dot(part(attended, section, False)[...], read_near[...])
    total = total + dot(part(attended, section, True)[...], read_far[...])
    residual[...] = total
    xhat, _ = nrm_stats(total)
    second[...] = (xhat * gain[...] + bias[...]).astype(LOW)


def feed_kernel(
    where, second, top, residual, gain, up_bias, up_near, up_far, down_near, down_far,
    act_near, act_far, lifted_t, up_bias_grad, output, residual_grad, residual_low, residual_t,
    gain_grad, bias_grad, out_sum, grad_sum,
):
    section = where[0]
    step, steps = pl.program_id(0), pl.num_programs(0)

    @pl.when(step == 0)
    def _():
        out_sum[...] = jnp.zeros_like(out_sum)
        grad_sum[...] = jnp.zeros_like(grad_sum)

    def run(down, act):
        lifted = dot(part(second, section, False)[...], up_near[...])
        lifted = lifted + dot(part(second, section, True)[...], up_far[...]) + up_bias[...]
        square = lifted * lifted
        turn = jnp.tanh(0.7978845608028654 * lifted * (1.0 + 0.044715 * square))
        rise = 0.5 * (1.0 + turn)
        slope = rise + (0.5 * 0.7978845608028654) * lifted * (1.0 - turn * turn) * (
            1.0 + 3 * 0.044715 * square
        )
        active = (lifted * rise).astype(LOW)
        act[...] = active
        out_sum[...] += dot(active, down[...])
        lifted_grad = (contract_last(top[...], down[...]) * slope).astype(LOW)
        wide = lifted_grad.astype(FULL)
        up_bias_grad[...] = jnp.sum(wide, axis=0, keepdims=True)
        lifted_t[...] = wide.T.astype(LOW)
        part(grad_sum, section, False)[...] += contract_last(lifted_grad, up_near[...])
        part(grad_sum, section, True)[...] += contract_last(lifted_grad, up_far[...])

    @pl.when(step < steps // 2)
    def _():
        run(down_near, act_near)

    @pl.when(step >= steps // 2)
    def _():
        run(down_far, act_far)

    @pl.when(step == steps - 1)
    def _():
        before = residual[...]
        output[...] = (before + out_sum[...]).astype(LOW)
        grad = grad_sum[...]
        xhat, scale = nrm_stats(before)
        gain_grad[...] = jnp.sum(grad * xhat, axis=0, keepdims=True)
        bias_grad[...] = jnp.sum(grad, axis=0, keepdims=True)
        total = top[...].astype(FULL) + nrm_back(xhat, scale, grad, gain[...])
        residual_grad[...] = total
        residual_low[...] = total.astype(LOW)
        residual_t[...] = total.T.astype(LOW)


def unattend_kernel(
    where, mixed, residual_low, seg_rows, seg_cols, read_near, read_far,
    mixed_grad, mixed_t, pulled,
):
    section = where[0]
    width = residual_low.shape[1]
    heads = width // HEAD_DIM
    grad = residual_low[...]
    part(pulled, section, False)[...] = contract_last(grad, read_near[...]).astype(LOW)
    part(pulled, section, True)[...] = contract_last(grad, read_far[...]).astype(LOW)
    same, apart, slopes, first = score_parts(heads, seg_rows[...], seg_cols[...])
    for two in range(heads // 2):
        spots = [slice(k * width + two * 128, k * width + two * 128 + 128) for k in range(3)]
        query, keys, values = (mixed[:, spot] for spot in spots)
        given = pulled[:, spots[0]]
        blank = jnp.zeros_like(query)
        made = []
        for head in (0, 1):
            keep = (lambda v: jnp.where(first, v, blank)) if head == 0 else (
                lambda v: jnp.where(first, blank, v)
            )
            probs = probs_of(keep(query), keys, slopes[2 * two + head], apart, same)
            prob_grad = contract_last(keep(given), values)
            score = probs * (prob_grad - jnp.sum(probs * prob_grad, -1, keepdims=True))
            score = score.astype(LOW)
            made.append(
                (
                    dot(score, keys) * 0.125,
                    contract_first(score, query) * 0.125,
                    contract_first(probs.astype(LOW), given),
                )
            )
        for spot, one, other in zip(spots, *made):
            both = jnp.where(first, one, other)
            mixed_grad[:, spot] = both.astype(LOW)
            mixed_t[spot, :] = both.T.astype(LOW)


def unmix_kernel(
    where, mixed_grad, mix_near, mix_far, merged, residual_grad, gain,
    merged_low, merged_t, gain_grad, bias_grad, first_grad,
):
    section = where[0]
    part(first_grad, section, False)[...] = contract_last(mixed_grad[...], mix_near[...])
    part(first_grad, section, True)[...] = contract_last(mixed_grad[...], mix_far[...])
    grad = first_grad[...]
    xhat, scale = nrm_stats(merged[...])
    gain_grad[...] = jnp.sum(grad * xhat, axis=0, keepdims=True)
    bias_grad[...] = jnp.sum(grad, axis=0, keepdims=True)
    total = residual_grad[...] + nrm_back(xhat, scale, grad, gain[...])
    merged_low[...] = total.astype(LOW)
    merged_t[...] = total.T.astype(LOW)


def unmerge_kernel(merged_low, near_w, far_w, near_grad, far_grad):
    near_grad[...] = contract_last(merged_low[...], near_w[...]).astype(LOW)
    far_grad[...] = contract_last(merged_low[...], far_w[...]).astype(LOW)


def shaped(shape, kind):
    return jax.ShapeDtypeStruct(shape, kind)


def plain_call(name, kernel, made, operands, scratch=(), scalars=0):
    cost = sum(x.size * x.dtype.itemsize for x in operands)
    specs = [pl.BlockSpec(memory_space=pltpu.SMEM)] * scalars
    specs += [pl.BlockSpec(memory_space=pltpu.VMEM)] * (len(operands) - scalars)
    with jax.named_scope(name):
        return pl.pallas_call(
            kernel,
            out_shape=made,
            in_specs=specs,
            out_specs=[pl.BlockSpec(memory_space=pltpu.VMEM)] * len(made),
            scratch_shapes=list(scratch),
            compiler_params=pltpu.CompilerParams(vmem_limit_bytes=56 << 20),
            cost_estimate=pl.CostEstimate(
                flops=128 * cost, bytes_accessed=cost, transcendentals=0
            ),
            name=name,
        )(*operands)


def feed_call(where, second, top, residual, gain, up_bias, up_near, up_far, down_near, down_far):
    rows, width = second.shape
    hidden = up_near.shape[1]
    steps = 8
    tile, last = hidden // steps, steps // 2 - 1
    half = width // 2

    def whole(*shape):
        return pl.BlockSpec(shape, lambda j, w: (0,) * len(shape))

    def spot(j, w):
        return (j // (steps // 2) + w[0]) % 2 * (steps // 2) + j % (steps // 2)

    def near(j):
        return jnp.minimum(j, last)

    def far(j):
        return jnp.maximum(j - last - 1, 0)

    in_specs = [
        whole(rows, width), whole(rows, width), whole(rows, width), whole(1, width),
        pl.BlockSpec((1, tile), lambda j, w: (0, spot(j, w))),
        pl.BlockSpec((half, tile), lambda j, w: (0, spot(j, w))),
        pl.BlockSpec((half, tile), lambda j, w: (0, spot(j, w))),
        pl.BlockSpec((tile, width), lambda j, w: (near(j), 0)),
        pl.BlockSpec((tile, width), lambda j, w: (far(j), 0)),
    ]
    out_specs = [
        pl.BlockSpec((rows, tile), lambda j, w: (0, near(j))),
        pl.BlockSpec((rows, tile), lambda j, w: (0, far(j))),
        pl.BlockSpec((tile, rows), lambda j, w: (spot(j, w), 0)),
        pl.BlockSpec((1, tile), lambda j, w: (0, spot(j, w))),
        whole(rows, width), whole(rows, width), whole(rows, width), whole(width, rows),
        whole(1, width), whole(1, width),
    ]
    made = [
        shaped((rows, hidden // 2), LOW), shaped((rows, hidden // 2), LOW),
        shaped((hidden, rows), LOW), shaped((1, hidden), FULL),
        shaped((rows, width), LOW), shaped((rows, width), FULL), shaped((rows, width), LOW),
        shaped((width, rows), LOW), shaped((1, width), FULL), shaped((1, width), FULL),
    ]
    weights = 4 * width * hidden
    with jax.named_scope("feed"):
        return pl.pallas_call(
            feed_kernel,
            out_shape=made,
            grid_spec=pltpu.PrefetchScalarGridSpec(
                num_scalar_prefetch=1,
                grid=(steps,),
                in_specs=in_specs,
                out_specs=out_specs,
                scratch_shapes=[pltpu.VMEM((rows, width), FULL)] * 2,
            ),
            compiler_params=pltpu.CompilerParams(
                dimension_semantics=("arbitrary",), vmem_limit_bytes=56 << 20
            ),
            cost_estimate=pl.CostEstimate(
                flops=4 * rows * weights, bytes_accessed=weights, transcendentals=rows * hidden
            ),
            name="feed",
        )(where, second, top, residual, gain, up_bias, up_near, up_far, down_near, down_far)


def pick(value, spot, axis=0):
    return lax.dynamic_index_in_dim(value, spot, axis, keepdims=False)


def gather_left(torus, axis, own, far):
    chip = jnp.concatenate([own, far], axis=0)
    return jnp.concatenate([chip, torus.flip(chip, torus.order(axis)[0])], axis=0)


def gather_right(torus, axis, own):
    lead, rest = torus.order(axis)
    columns, tokens = own.shape
    split = own.reshape(*(2,) * torus.power, columns // torus.count, tokens)
    place = [torus.power - 1 - bit for bit in (lead, *rest)]
    split = split.transpose(*place, torus.power, torus.power + 1)
    split = split.reshape(2, columns // 2, tokens)
    here = torus.bit(lead)
    near = jnp.stack([pick(split, here), torus.flip(pick(split, 1 - here), lead)])
    far = pair(near)
    return jnp.concatenate([near[0], far[0], near[1], far[1]], axis=1)


def reduce_grad(torus, axis, left, right):
    rest = torus.order(axis)[1]
    halves = right.reshape(2, -1, right.shape[1])
    here = torus.bit(rest[0])
    sent = torus.flip(dot(pick(halves, 1 - here), left).astype(LOW), rest[0])
    total = dot(pick(halves, here), left) + sent.astype(FULL)
    for bit in rest[1:]:
        here = torus.bit(bit)
        held = total.astype(LOW).reshape(2, -1, left.shape[1])
        total = pick(held, here).astype(FULL) + torus.flip(pick(held, 1 - here), bit).astype(FULL)
    return total


def body(
    layer_input,
    skip_input,
    segment_ids,
    out_cotangent,
    merger,
    mixing,
    readout,
    expand,
    narrow,
    first_gain,
    first_bias,
    second_gain,
    second_bias,
    up_bias,
):
    torus = Torus(lax.axis_size("dp"))
    section = lax.axis_index("section")
    rows, width = layer_input.shape
    first_core = section == 0

    def mine(value):
        half = value.shape[1] // 2
        return lax.dynamic_slice_in_dim(value, section * half, half, 1)

    def other(value):
        half = value.shape[1] // 2
        return lax.dynamic_slice_in_dim(value, (1 - section) * half, half, 1)

    def joined(own, far, axis):
        return jnp.where(
            first_core,
            jnp.concatenate([own, far], axis=axis),
            jnp.concatenate([far, own], axis=axis),
        )

    merger_far = pair(merger)
    vectors = jnp.concatenate([first_gain, first_bias, second_gain, second_bias, up_bias])
    vectors_far = pair(vectors)
    mixing_far = pair(mixing)
    readout_far = pair(readout)
    expand_far = pair(expand)
    narrow_far = pair(narrow)

    bounds = []
    start = 0
    for vector in (first_gain, first_bias, second_gain, second_bias, up_bias):
        bounds.append((start, start + vector.shape[0]))
        start += vector.shape[0]
    gain_one, bias_one, gain_two, bias_two, bias_up = (
        joined(vectors[low:high], vectors_far[low:high], 0).astype(FULL)[None] for low, high in bounds
    )

    where = section.astype(jnp.int32).reshape(1)
    frames_mine = jnp.where(first_core, layer_input, skip_input)
    frames_other = jnp.where(first_core, skip_input, layer_input)
    segments = pick(segment_ids[0], section)
    seg_rows, seg_cols = segments[:, None], segments[None, :]
    top_low = pair(out_cotangent)
    flat, tall = (rows, width), (width, rows)
    line = shaped((1, width), FULL)

    merged, first_low = plain_call(
        "merge", merge_kernel, [shaped(flat, FULL), shaped(flat, LOW)],
        (frames_mine, frames_other, merger, merger_far, gain_one, bias_one),
    )
    mixed, attended, residual, second_low = plain_call(
        "attend", attend_kernel,
        [shaped((rows, 3 * width), LOW), shaped(flat, LOW), shaped(flat, FULL), shaped(flat, LOW)],
        (where, first_low, merged, seg_rows, seg_cols, mixing, mixing_far, readout, readout_far,
         gain_two, bias_two),
        scalars=1,
    )
    (act_near, act_far, lifted_t, up_bias_grad, output, residual_grad, residual_low, residual_t,
     second_gain_grad, second_bias_grad) = feed_call(
        where, second_low, top_low, residual, gain_two, bias_up, expand, expand_far, narrow,
        narrow_far,
    )
    block_output = pair(output)
    mixed_grad, mixed_t = plain_call(
        "unattend", unattend_kernel,
        [shaped((rows, 3 * width), LOW), shaped((3 * width, rows), LOW)],
        (where, mixed, residual_low, seg_rows, seg_cols, readout, readout_far),
        scratch=[pltpu.VMEM(flat, LOW)], scalars=1,
    )
    merged_low, merged_t, first_gain_grad, first_bias_grad = plain_call(
        "unmix", unmix_kernel, [shaped(flat, LOW), shaped(tall, LOW), line, line],
        (where, mixed_grad, mixing, mixing_far, merged, residual_grad, gain_one),
        scratch=[pltpu.VMEM(flat, FULL)], scalars=1,
    )
    near_grad, far_grad = plain_call(
        "unmerge", unmerge_kernel, [shaped(flat, LOW)] * 2, (merged_low, merger, merger_far)
    )
    input_grad = jnp.where(first_core, near_grad, far_grad)
    skip_grad = jnp.where(first_core, far_grad, near_grad)

    def grad_of(axis, own, far, right_t):
        left = gather_left(torus, axis, own, pair(far))
        return reduce_grad(torus, axis, left, gather_right(torus, axis, right_t))

    narrow_grad = grad_of("x", act_near, act_far, top_low.T)
    expand_grad = grad_of("y", mine(second_low), other(second_low), lifted_t)
    readout_grad = grad_of("y", mine(attended), other(attended), residual_t)
    mixing_grad = grad_of("y", mine(first_low), other(first_low), mixed_t)
    merger_grad = grad_of("x", frames_mine, frames_other, merged_t)

    keep, give = [], []
    for line in (first_gain_grad, first_bias_grad, second_gain_grad, second_bias_grad, up_bias_grad):
        keep.append(mine(line)[0])
        give.append(other(line)[0])
    small = jnp.concatenate(keep) + pair(jnp.concatenate(give))
    small = small.reshape(-1, 128)
    for bit in range(torus.power):
        small = small + torus.flip(small, bit)
    small = small.reshape(-1)
    matrices = tuple(
        grad.T for grad in (merger_grad, mixing_grad, readout_grad, expand_grad, narrow_grad)
    )
    return (block_output, input_grad, skip_grad) + matrices + tuple(
        small[low:high] for low, high in bounds
    )


def solution(mesh):
    tokens = P(("section", "dp"), None)
    matrix, vector = P("section", None), P("section")
    placed = (tokens, tokens, P("dp", None, None), tokens) + (matrix,) * 5 + (vector,) * 5
    made = (tokens,) * 3 + (P("section", "dp"),) * 5 + (vector,) * 5
    return jax.shard_map(body, mesh=mesh, in_specs=placed, out_specs=made, check_vma=False)
```

```python
import jax
import jax.numpy as jnp
from jax import lax
from jax.experimental import pallas as pl
from jax.experimental.pallas import tpu as pltpu
from jax.sharding import PartitionSpec as P


HEAD_DIM = 64
LOW = jnp.bfloat16
FULL = jnp.float32


class Torus:
    def __init__(self, count):
        power = count.bit_length() - 1
        side = power // 3
        self.count, self.power = count, power
        self.bits = {
            "x": list(range(side)),
            "y": list(range(side, 2 * side)),
            "z": list(range(2 * side, power)),
        }

    def order(self, axis):
        lead = self.bits[axis]
        across = self.bits["y" if axis == "x" else "x"]
        return lead[0], across + lead[1:] + self.bits["z"]

    def bit(self, bit):
        return (lax.axis_index("dp") >> bit) & 1

    def flip(self, value, bit):
        pairs = [(source, source ^ (1 << bit)) for source in range(self.count)]
        return lax.ppermute(value, "dp", pairs)


def pair(value):
    return lax.ppermute(value, "section", [(0, 1), (1, 0)])


def dot(left, right):
    return jnp.dot(left, right, preferred_element_type=FULL)


def contract_first(left, right):
    return lax.dot_general(left, right, (((0,), (0,)), ((), ())), preferred_element_type=FULL)


def contract_last(left, right):
    return lax.dot_general(left, right, (((1,), (1,)), ((), ())), preferred_element_type=FULL)


def nrm_stats(values):
    center = values - jnp.mean(values, -1, keepdims=True)
    scale = lax.rsqrt(jnp.mean(center * center, -1, keepdims=True) + 1e-05)
    return center * scale, scale


def nrm_back(xhat, scale, grad, gain):
    g = grad * gain
    inner = g - jnp.mean(g, -1, keepdims=True) - xhat * jnp.mean(g * xhat, -1, keepdims=True)
    return scale * inner


def part(ref, section, far):
    half = ref.shape[1] // 2
    spot = (1 - section) if far else section
    return ref.at[:, pl.ds(pl.multiple_of(spot * half, half), half)]


def vector(section, near, far, low, size):
    one, two = near[:, low : low + size].astype(FULL), far[:, low : low + size].astype(FULL)
    return jnp.where(
        section == 0, jnp.concatenate([one, two], axis=1), jnp.concatenate([two, one], axis=1)
    )


def merge_kernel(where, near_x, far_x, near_w, far_w, near_v, far_v, merged, low):
    half = near_x.shape[1] // 2
    gain = vector(where[0], near_v, far_v, 0, half)
    bias = vector(where[0], near_v, far_v, half, half)
    total = dot(near_x[...], near_w[...]) + dot(far_x[...], far_w[...])
    merged[...] = total
    xhat, _ = nrm_stats(total)
    low[...] = (xhat * gain + bias).astype(LOW)


def score_parts(heads, seg_rows, seg_cols):
    rows = seg_rows.shape[0]
    same = seg_rows == seg_cols
    spots = [lax.broadcasted_iota(jnp.int32, (rows, rows), axis) for axis in (0, 1)]
    apart = jnp.abs(spots[0] - spots[1]).astype(FULL)
    slopes = [2.0 ** (-8.0 * (head + 1) / heads) for head in range(heads)]
    lane = lax.broadcasted_iota(jnp.int32, (rows, 2 * HEAD_DIM), 1)
    return same, apart, slopes, lane < HEAD_DIM


def probs_of(query, keys, slope, apart, same):
    raw = contract_last(query, keys) * 0.125 - slope * apart
    raw = jnp.where(same, raw, -1000000000.0)
    raised = jnp.exp(raw - jnp.max(raw, -1, keepdims=True))
    return raised / jnp.sum(raised, -1, keepdims=True)


def attend_kernel(
    where, low, merged, seg_rows, seg_cols, mix_near, mix_far, read_near, read_far, near_v, far_v,
    mixed, attended, residual, second,
):
    section = where[0]
    width = low.shape[1]
    heads = width // HEAD_DIM
    near, far = part(low, section, False)[...], part(low, section, True)[...]
    step = width // 2
    for base in range(0, 3 * width, step):
        block = dot(near, mix_near[:, base : base + step]) + dot(far, mix_far[:, base : base + step])
        mixed[:, base : base + step] = block.astype(LOW)
    same, apart, slopes, first = score_parts(heads, seg_rows[...], seg_cols[...])
    for two in range(heads // 2):
        lanes = slice(two * 128, two * 128 + 128)
        query = mixed[:, lanes]
        keys = mixed[:, width + two * 128 : width + two * 128 + 128]
        values = mixed[:, 2 * width + two * 128 : 2 * width + two * 128 + 128]
        blank = jnp.zeros_like(query)
        outs = []
        for head in (0, 1):
            own = jnp.where(first, query, blank) if head == 0 else jnp.where(first, blank, query)
            probs = probs_of(own, keys, slopes[2 * two + head], apart, same)
            outs.append(dot(probs.astype(LOW), values))
        attended[:, lanes] = jnp.where(first, outs[0], outs[1]).astype(LOW)
    total = merged[...] + dot(part(attended, section, False)[...], read_near[...])
    total = total + dot(part(attended, section, True)[...], read_far[...])
    residual[...] = total
    xhat, _ = nrm_stats(total)
    gain = vector(section, near_v, far_v, width, width // 2)
    bias = vector(section, near_v, far_v, width + width // 2, width // 2)
    second[...] = (xhat * gain + bias).astype(LOW)


def feed_kernel(
    where, second, top, residual, near_v, far_v, up_near, up_far, down_near, down_far,
    act_near, act_far, lifted_t, up_bias_grad, output, residual_grad, residual_low, residual_t,
    gain_grad, bias_grad, out_sum, grad_sum,
):
    section = where[0]
    step, steps = pl.program_id(0), pl.num_programs(0)

    @pl.when(step == 0)
    def _():
        out_sum[...] = jnp.zeros_like(out_sum)
        grad_sum[...] = jnp.zeros_like(grad_sum)

    def run(down, act, packed):
        tile = up_near.shape[1]
        spot = pl.multiple_of(2 * second.shape[1] + step % (steps // 2) * tile, tile)
        up_bias = packed[:, pl.ds(spot, tile)].astype(FULL)
        lifted = dot(part(second, section, False)[...], up_near[...])
        lifted = lifted + dot(part(second, section, True)[...], up_far[...]) + up_bias
        square = lifted * lifted
        turn = jnp.tanh(0.7978845608028654 * lifted * (1.0 + 0.044715 * square))
        rise = 0.5 * (1.0 + turn)
        slope = rise + (0.5 * 0.7978845608028654) * lifted * (1.0 - turn * turn) * (
            1.0 + 3 * 0.044715 * square
        )
        active = (lifted * rise).astype(LOW)
        act[...] = active
        out_sum[...] += dot(active, down[...])
        lifted_grad = (contract_last(top[...], down[...]) * slope).astype(LOW)
        wide = lifted_grad.astype(FULL)
        up_bias_grad[...] = jnp.sum(wide, axis=0, keepdims=True)
        lifted_t[...] = wide.T.astype(LOW)
        part(grad_sum, section, False)[...] += contract_last(lifted_grad, up_near[...])
        part(grad_sum, section, True)[...] += contract_last(lifted_grad, up_far[...])

    @pl.when(step < steps // 2)
    def _():
        run(down_near, act_near, near_v)

    @pl.when(step >= steps // 2)
    def _():
        run(down_far, act_far, far_v)

    @pl.when(step == steps - 1)
    def _():
        before = residual[...]
        output[...] = (before + out_sum[...]).astype(LOW)
        grad = grad_sum[...]
        xhat, scale = nrm_stats(before)
        gain_grad[...] = jnp.sum(grad * xhat, axis=0, keepdims=True)
        bias_grad[...] = jnp.sum(grad, axis=0, keepdims=True)
        width = second.shape[1]
        gain = vector(section, near_v, far_v, width, width // 2)
        total = top[...].astype(FULL) + nrm_back(xhat, scale, grad, gain)
        residual_grad[...] = total
        residual_low[...] = total.astype(LOW)
        residual_t[...] = total.T.astype(LOW)


def unattend_kernel(
    where, mixed, residual_low, seg_rows, seg_cols, read_near, read_far,
    mixed_grad, mixed_t, pulled,
):
    section = where[0]
    width = residual_low.shape[1]
    heads = width // HEAD_DIM
    grad = residual_low[...]
    part(pulled, section, False)[...] = contract_last(grad, read_near[...]).astype(LOW)
    part(pulled, section, True)[...] = contract_last(grad, read_far[...]).astype(LOW)
    same, apart, slopes, first = score_parts(heads, seg_rows[...], seg_cols[...])
    for two in range(heads // 2):
        spots = [slice(k * width + two * 128, k * width + two * 128 + 128) for k in range(3)]
        query, keys, values = (mixed[:, spot] for spot in spots)
        given = pulled[:, spots[0]]
        blank = jnp.zeros_like(query)
        made = []
        for head in (0, 1):
            keep = (lambda v: jnp.where(first, v, blank)) if head == 0 else (
                lambda v: jnp.where(first, blank, v)
            )
            probs = probs_of(keep(query), keys, slopes[2 * two + head], apart, same)
            prob_grad = contract_last(keep(given), values)
            score = probs * (prob_grad - jnp.sum(probs * prob_grad, -1, keepdims=True))
            score = score.astype(LOW)
            made.append(
                (
                    dot(score, keys) * 0.125,
                    contract_first(score, query) * 0.125,
                    contract_first(probs.astype(LOW), given),
                )
            )
        for spot, one, other in zip(spots, *made):
            both = jnp.where(first, one, other)
            mixed_grad[:, spot] = both.astype(LOW)
            mixed_t[spot, :] = both.T.astype(LOW)


def unmix_kernel(
    where, mixed_grad, mix_near, mix_far, merged, residual_grad, near_v, far_v,
    merged_low, merged_t, gain_grad, bias_grad, first_grad,
):
    section = where[0]
    part(first_grad, section, False)[...] = contract_last(mixed_grad[...], mix_near[...])
    part(first_grad, section, True)[...] = contract_last(mixed_grad[...], mix_far[...])
    grad = first_grad[...]
    xhat, scale = nrm_stats(merged[...])
    gain_grad[...] = jnp.sum(grad * xhat, axis=0, keepdims=True)
    bias_grad[...] = jnp.sum(grad, axis=0, keepdims=True)
    gain = vector(section, near_v, far_v, 0, merged.shape[1] // 2)
    total = residual_grad[...] + nrm_back(xhat, scale, grad, gain)
    merged_low[...] = total.astype(LOW)
    merged_t[...] = total.T.astype(LOW)


def unmerge_kernel(merged_low, near_w, far_w, near_grad, far_grad):
    near_grad[...] = contract_last(merged_low[...], near_w[...]).astype(LOW)
    far_grad[...] = contract_last(merged_low[...], far_w[...]).astype(LOW)


def shaped(shape, kind):
    return jax.ShapeDtypeStruct(shape, kind)


def plain_call(kernel, made, operands, scratch=(), scalars=0):
    cost = sum(x.size * x.dtype.itemsize for x in operands)
    specs = [pl.BlockSpec(memory_space=pltpu.SMEM)] * scalars
    specs += [pl.BlockSpec(memory_space=pltpu.VMEM)] * (len(operands) - scalars)
    return pl.pallas_call(
        kernel,
        out_shape=made,
        in_specs=specs,
        out_specs=[pl.BlockSpec(memory_space=pltpu.VMEM)] * len(made),
        scratch_shapes=list(scratch),
        compiler_params=pltpu.CompilerParams(vmem_limit_bytes=56 << 20),
        cost_estimate=pl.CostEstimate(
            flops=128 * cost, bytes_accessed=cost, transcendentals=0
        ),
    )(*operands)


def feed_call(where, second, top, residual, near_v, far_v, up_near, up_far, down_near, down_far):
    rows, width = second.shape
    hidden = up_near.shape[1]
    steps = 8
    tile, last = hidden // steps, steps // 2 - 1
    half = width // 2

    def whole(*shape):
        return pl.BlockSpec(shape, lambda j, w: (0,) * len(shape))

    def spot(j, w):
        return (j // (steps // 2) + w[0]) % 2 * (steps // 2) + j % (steps // 2)

    def near(j):
        return jnp.minimum(j, last)

    def far(j):
        return jnp.maximum(j - last - 1, 0)

    in_specs = [
        whole(rows, width), whole(rows, width), whole(rows, width),
        whole(*near_v.shape), whole(*far_v.shape),
        pl.BlockSpec((half, tile), lambda j, w: (0, spot(j, w))),
        pl.BlockSpec((half, tile), lambda j, w: (0, spot(j, w))),
        pl.BlockSpec((tile, width), lambda j, w: (near(j), 0)),
        pl.BlockSpec((tile, width), lambda j, w: (far(j), 0)),
    ]
    out_specs = [
        pl.BlockSpec((rows, tile), lambda j, w: (0, near(j))),
        pl.BlockSpec((rows, tile), lambda j, w: (0, far(j))),
        pl.BlockSpec((tile, rows), lambda j, w: (spot(j, w), 0)),
        pl.BlockSpec((1, tile), lambda j, w: (0, spot(j, w))),
        whole(rows, width), whole(rows, width), whole(rows, width), whole(width, rows),
        whole(1, width), whole(1, width),
    ]
    made = [
        shaped((rows, hidden // 2), LOW), shaped((rows, hidden // 2), LOW),
        shaped((hidden, rows), LOW), shaped((1, hidden), FULL),
        shaped((rows, width), LOW), shaped((rows, width), FULL), shaped((rows, width), LOW),
        shaped((width, rows), LOW), shaped((1, width), FULL), shaped((1, width), FULL),
    ]
    weights = 4 * width * hidden
    return pl.pallas_call(
        feed_kernel,
        out_shape=made,
        grid_spec=pltpu.PrefetchScalarGridSpec(
            num_scalar_prefetch=1,
            grid=(steps,),
            in_specs=in_specs,
            out_specs=out_specs,
            scratch_shapes=[pltpu.VMEM((rows, width), FULL)] * 2,
        ),
        compiler_params=pltpu.CompilerParams(
            dimension_semantics=("arbitrary",), vmem_limit_bytes=56 << 20
        ),
        cost_estimate=pl.CostEstimate(
            flops=4 * rows * weights, bytes_accessed=weights, transcendentals=rows * hidden
        ),
        name="feed",
    )(where, second, top, residual, near_v, far_v, up_near, up_far, down_near, down_far)


def pick(value, spot, axis=0):
    return lax.dynamic_index_in_dim(value, spot, axis, keepdims=False)


def gather_left(torus, axis, own, far):
    chip = jnp.concatenate([own, far], axis=0)
    lead = torus.order(axis)[0]
    return jnp.concatenate([chip, torus.flip(chip, lead)], axis=0)


def gather_right(torus, axis, own):
    lead, rest = torus.order(axis)
    columns, tokens = own.shape
    split = own.reshape(*(2,) * torus.power, columns // torus.count, tokens)
    place = [torus.power - 1 - bit for bit in (lead, *rest)]
    split = split.transpose(*place, torus.power, torus.power + 1)
    split = split.reshape(2, columns // 2, tokens)
    here = torus.bit(lead)
    near = jnp.stack([pick(split, here), torus.flip(pick(split, 1 - here), lead)])
    far = pair(near)
    return jnp.concatenate([near[0], far[0], near[1], far[1]], axis=1)


def reduce_grad(torus, axis, left, right):
    rest = torus.order(axis)[1]
    halves = right.reshape(2, -1, right.shape[1])
    here = torus.bit(rest[0])
    sent = dot(pick(halves, 1 - here), left).astype(LOW)
    sent = torus.flip(sent, rest[0])
    total = dot(pick(halves, here), left) + sent.astype(FULL)
    for bit in rest[1:]:
        here = torus.bit(bit)
        held = total.astype(LOW).reshape(2, -1, left.shape[1])
        sent = torus.flip(pick(held, 1 - here), bit)
        total = pick(held, here).astype(FULL) + sent.astype(FULL)
    return total


def body(
    layer_input,
    skip_input,
    segment_ids,
    out_cotangent,
    merger,
    mixing,
    readout,
    expand,
    narrow,
    first_gain,
    first_bias,
    second_gain,
    second_bias,
    up_bias,
):
    torus = Torus(lax.axis_size("dp"))
    section = lax.axis_index("section")
    rows, width = layer_input.shape
    first_core = section == 0

    def packed(parts):
        bounds, total = [], 0
        for item in parts:
            bounds.append((total, total + item.shape[0]))
            total += item.shape[0]
        placed = [jnp.pad(item, (low, total - high)) for item, (low, high) in zip(parts, bounds)]
        return sum(placed[1:], placed[0]), bounds

    def mine(value):
        half = value.shape[-1] // 2
        return lax.dynamic_slice_in_dim(value, section * half, half, value.ndim - 1)

    def other(value):
        half = value.shape[-1] // 2
        return lax.dynamic_slice_in_dim(value, (1 - section) * half, half, value.ndim - 1)

    merger_far = pair(merger)
    near_v, _ = packed((first_gain, first_bias, second_gain, second_bias, up_bias))
    near_v = near_v[None]
    far_v = pair(near_v)
    mixing_far = pair(mixing)
    readout_far = pair(readout)
    expand_far = pair(expand)
    narrow_far = pair(narrow)
    top_low = pair(out_cotangent)

    where = section.astype(jnp.int32).reshape(1)
    frames_mine = jnp.where(first_core, layer_input, skip_input)
    frames_other = jnp.where(first_core, skip_input, layer_input)
    segments = pick(segment_ids[0], section)
    seg_rows, seg_cols = segments[:, None], segments[None, :]
    flat, tall = (rows, width), (width, rows)
    line = shaped((1, width), FULL)

    merged, first_low = plain_call(
        merge_kernel, [shaped(flat, FULL), shaped(flat, LOW)],
        (where, frames_mine, frames_other, merger, merger_far, near_v, far_v), scalars=1,
    )
    mixed, attended, residual, second_low = plain_call(
        attend_kernel,
        [shaped((rows, 3 * width), LOW), shaped(flat, LOW), shaped(flat, FULL), shaped(flat, LOW)],
        (where, first_low, merged, seg_rows, seg_cols, mixing, mixing_far, readout, readout_far,
         near_v, far_v),
        scalars=1,
    )
    (act_near, act_far, lifted_t, up_bias_grad, output, residual_grad, residual_low, residual_t,
     second_gain_grad, second_bias_grad) = feed_call(
        where, second_low, top_low, residual, near_v, far_v, expand, expand_far, narrow, narrow_far
    )
    block_output = pair(output)
    mixed_grad, mixed_t = plain_call(
        unattend_kernel,
        [shaped((rows, 3 * width), LOW), shaped((3 * width, rows), LOW)],
        (where, mixed, residual_low, seg_rows, seg_cols, readout, readout_far),
        scratch=[pltpu.VMEM(flat, LOW)], scalars=1,
    )
    merged_low, merged_t, first_gain_grad, first_bias_grad = plain_call(
        unmix_kernel, [shaped(flat, LOW), shaped(tall, LOW), line, line],
        (where, mixed_grad, mixing, mixing_far, merged, residual_grad, near_v, far_v),
        scratch=[pltpu.VMEM(flat, FULL)], scalars=1,
    )
    near_grad, far_grad = plain_call(
        unmerge_kernel, [shaped(flat, LOW)] * 2, (merged_low, merger, merger_far)
    )
    input_grad = jnp.where(first_core, near_grad, far_grad)
    skip_grad = jnp.where(first_core, far_grad, near_grad)

    def grad_of(axis, own, far, right_t):
        left = gather_left(torus, axis, own, pair(far))
        return reduce_grad(torus, axis, left, gather_right(torus, axis, right_t))

    narrow_grad = grad_of("x", act_near, act_far, top_low.T)
    expand_grad = grad_of("y", mine(second_low), other(second_low), lifted_t)
    readout_grad = grad_of("y", mine(attended), other(attended), residual_t)
    mixing_grad = grad_of("y", mine(first_low), other(first_low), mixed_t)
    merger_grad = grad_of("x", frames_mine, frames_other, merged_t)

    small, bounds = packed(
        [
            item[0]
            for item in (
                first_gain_grad, first_bias_grad, second_gain_grad, second_bias_grad, up_bias_grad
            )
        ]
    )
    small = small.reshape(-1, 128)
    small = small + pair(small)
    for bit in range(torus.power):
        small = small + torus.flip(small, bit)
    small = small.reshape(-1)
    matrices = tuple(
        grad.T for grad in (merger_grad, mixing_grad, readout_grad, expand_grad, narrow_grad)
    )
    return (block_output, input_grad, skip_grad) + matrices + tuple(
        mine(small[low:high]) for low, high in bounds
    )


def solution(mesh):
    tokens = P(("section", "dp"), None)
    matrix, vector = P("section", None), P("section")
    placed = (tokens, tokens, P("dp", None, None), tokens) + (matrix,) * 5 + (vector,) * 5
    made = (tokens,) * 3 + (P("section", "dp"),) * 5 + (vector,) * 5
    return jax.shard_map(body, mesh=mesh, in_specs=placed, out_specs=made, check_vma=False)
```

```python
import jax
import jax.numpy as jnp
from jax import lax
from jax.experimental import pallas as pl
from jax.experimental.pallas import tpu as pltpu
from jax.sharding import PartitionSpec as P


HEAD_DIM = 64
LOW = jnp.bfloat16
FULL = jnp.float32


class Torus:
    def __init__(self, count):
        power = count.bit_length() - 1
        side = power // 3
        self.count, self.power = count, power
        self.bits = {
            "x": list(range(side)),
            "y": list(range(side, 2 * side)),
            "z": list(range(2 * side, power)),
        }

    def order(self, axes):
        lead = self.bits[axes[0]]
        return lead[0], self.bits[axes[1]] + self.bits[axes[2]] + lead[1:]

    def bit(self, bit):
        return (lax.axis_index("dp") >> bit) & 1

    def flip(self, value, bit):
        pairs = [(source, source ^ (1 << bit)) for source in range(self.count)]
        return lax.ppermute(value, "dp", pairs)


def pair(value):
    return lax.ppermute(value, "section", [(0, 1), (1, 0)])


def dot(left, right):
    return jnp.dot(left, right, preferred_element_type=FULL)


def contract_first(left, right):
    return lax.dot_general(left, right, (((0,), (0,)), ((), ())), preferred_element_type=FULL)


def contract_last(left, right):
    return lax.dot_general(left, right, (((1,), (1,)), ((), ())), preferred_element_type=FULL)


def nrm_stats(values):
    center = values - jnp.mean(values, -1, keepdims=True)
    scale = lax.rsqrt(jnp.mean(center * center, -1, keepdims=True) + 1e-05)
    return center * scale, scale


def nrm_back(xhat, scale, grad, gain):
    g = grad * gain
    inner = g - jnp.mean(g, -1, keepdims=True) - xhat * jnp.mean(g * xhat, -1, keepdims=True)
    return scale * inner


def part(ref, section, far):
    half = ref.shape[1] // 2
    spot = (1 - section) if far else section
    return ref.at[:, pl.ds(pl.multiple_of(spot * half, half), half)]


def vector(section, near, far, low, size):
    one, two = near[:, low : low + size].astype(FULL), far[:, low : low + size].astype(FULL)
    return jnp.where(
        section == 0, jnp.concatenate([one, two], axis=1), jnp.concatenate([two, one], axis=1)
    )


def halves(section, values, near, far):
    half = values.shape[1] // 2
    one, two = values[:, :half], values[:, half:]
    near[...] = jnp.where(section == 0, one, two)
    far[...] = jnp.where(section == 0, two, one)


def merge_kernel(
    where, first_x, second_x, near_w, far_w, near_v, far_v, merged, low_near, low_far
):
    half = first_x.shape[1] // 2
    near_x = jnp.where(where[0] == 0, first_x[...], second_x[...])
    far_x = jnp.where(where[0] == 0, second_x[...], first_x[...])
    gain = vector(where[0], near_v, far_v, 0, half)
    bias = vector(where[0], near_v, far_v, half, half)
    total = dot(near_x, near_w[...]) + dot(far_x, far_w[...])
    merged[...] = total
    xhat, _ = nrm_stats(total)
    halves(where[0], (xhat * gain + bias).astype(LOW), low_near, low_far)


def score_parts(heads, segments):
    rows = segments.shape[1]
    spread = jnp.broadcast_to(segments.astype(FULL), (rows, rows))
    same = spread == spread.T
    spots = [lax.broadcasted_iota(jnp.int32, (rows, rows), axis) for axis in (0, 1)]
    apart = jnp.abs(spots[0] - spots[1]).astype(FULL)
    slopes = [2.0 ** (-8.0 * (head + 1) / heads) for head in range(heads)]
    lane = lax.broadcasted_iota(jnp.int32, (rows, 2 * HEAD_DIM), 1)
    return same, apart, slopes, lane < HEAD_DIM


def probs_of(query, keys, slope, apart, same):
    raw = contract_last(query, keys) * 0.125 - slope * apart
    raw = jnp.where(same, raw, -1000000000.0)
    raised = jnp.exp(raw - jnp.max(raw, -1, keepdims=True))
    return raised / jnp.sum(raised, -1, keepdims=True)


def attend_kernel(
    where, near_low, far_low, merged, segments, mix_near, mix_far, read_near, read_far, near_v, far_v,
    mixed, pack_near, pack_far, residual, attended,
):
    section = where[0]
    width = merged.shape[1]
    heads = width // HEAD_DIM
    near, far = near_low[...], far_low[...]
    step = width // 2
    for base in range(0, 3 * width, step):
        block = dot(near, mix_near[:, base : base + step]) + dot(far, mix_far[:, base : base + step])
        mixed[:, base : base + step] = block.astype(LOW)
    same, apart, slopes, first = score_parts(heads, segments[...])
    for two in range(heads // 2):
        lanes = slice(two * 128, two * 128 + 128)
        query = mixed[:, lanes]
        keys = mixed[:, width + two * 128 : width + two * 128 + 128]
        values = mixed[:, 2 * width + two * 128 : 2 * width + two * 128 + 128]
        blank = jnp.zeros_like(query)
        outs = []
        for head in (0, 1):
            own = jnp.where(first, query, blank) if head == 0 else jnp.where(first, blank, query)
            probs = probs_of(own, keys, slopes[2 * two + head], apart, same)
            outs.append(dot(probs.astype(LOW), values))
        attended[:, lanes] = jnp.where(first, outs[0], outs[1]).astype(LOW)
    half = width // 2
    halves(section, attended[...], pack_near.at[:, :half], pack_far.at[:, :half])
    total = merged[...] + dot(pack_near[:, :half], read_near[...])
    total = total + dot(pack_far[:, :half], read_far[...])
    residual[...] = total
    xhat, _ = nrm_stats(total)
    gain = vector(section, near_v, far_v, width, width // 2)
    bias = vector(section, near_v, far_v, width + width // 2, width // 2)
    second = (xhat * gain + bias).astype(LOW)
    halves(section, second, pack_near.at[:, half:], pack_far.at[:, half:])


def feed_kernel(
    where, pack_near, pack_far, top, residual, near_v, far_v, up_near, up_far, down_near, down_far,
    act_near, act_far, lifted_t, up_bias_grad, output, residual_grad, residual_low, residual_t,
    gain_grad, bias_grad, out_sum, grad_sum,
):
    section = where[0]
    step, steps = pl.program_id(0), pl.num_programs(0)

    @pl.when(step == 0)
    def _():
        out_sum[...] = jnp.zeros_like(out_sum)
        grad_sum[...] = jnp.zeros_like(grad_sum)

    def run(down, act, packed):
        tile = up_near.shape[1]
        spot = pl.multiple_of(2 * top.shape[1] + step % (steps // 2) * tile, tile)
        up_bias = packed[:, pl.ds(spot, tile)].astype(FULL)
        half = pack_near.shape[1] // 2
        lifted = dot(pack_near[:, half:], up_near[...])
        lifted = lifted + dot(pack_far[:, half:], up_far[...]) + up_bias
        square = lifted * lifted
        turn = jnp.tanh(0.7978845608028654 * lifted * (1.0 + 0.044715 * square))
        rise = 0.5 * (1.0 + turn)
        slope = rise + (0.5 * 0.7978845608028654) * lifted * (1.0 - turn * turn) * (
            1.0 + 3 * 0.044715 * square
        )
        active = (lifted * rise).astype(LOW)
        act[...] = active
        out_sum[...] += dot(active, down[...])
        lifted_grad = (contract_last(top[...], down[...]) * slope).astype(LOW)
        wide = lifted_grad.astype(FULL)
        up_bias_grad[...] = jnp.sum(wide, axis=0, keepdims=True)
        lifted_t[...] = wide.T.astype(LOW)
        part(grad_sum, section, False)[...] += contract_last(lifted_grad, up_near[...])
        part(grad_sum, section, True)[...] += contract_last(lifted_grad, up_far[...])

    @pl.when(step < steps // 2)
    def _():
        run(down_near, act_near, near_v)

    @pl.when(step >= steps // 2)
    def _():
        run(down_far, act_far, far_v)

    @pl.when(step == steps - 1)
    def _():
        before = residual[...]
        output[...] = (before + out_sum[...]).astype(LOW)
        grad = grad_sum[...]
        xhat, scale = nrm_stats(before)
        gain_grad[...] = jnp.sum(grad * xhat, axis=0, keepdims=True)
        bias_grad[...] = jnp.sum(grad, axis=0, keepdims=True)
        width = top.shape[1]
        gain = vector(section, near_v, far_v, width, width // 2)
        total = top[...].astype(FULL) + nrm_back(xhat, scale, grad, gain)
        residual_grad[...] = total
        residual_low[...] = total.astype(LOW)
        residual_t[...] = total.T.astype(LOW)


def unattend_kernel(
    where, mixed, residual_low, segments, read_near, read_far,
    mixed_grad, mixed_t, pulled,
):
    section = where[0]
    width = residual_low.shape[1]
    heads = width // HEAD_DIM
    grad = residual_low[...]
    part(pulled, section, False)[...] = contract_last(grad, read_near[...]).astype(LOW)
    part(pulled, section, True)[...] = contract_last(grad, read_far[...]).astype(LOW)
    same, apart, slopes, first = score_parts(heads, segments[...])
    for two in range(heads // 2):
        spots = [slice(k * width + two * 128, k * width + two * 128 + 128) for k in range(3)]
        query, keys, values = (mixed[:, spot] for spot in spots)
        given = pulled[:, spots[0]]
        blank = jnp.zeros_like(query)
        made = []
        for head in (0, 1):
            keep = (lambda v: jnp.where(first, v, blank)) if head == 0 else (
                lambda v: jnp.where(first, blank, v)
            )
            probs = probs_of(keep(query), keys, slopes[2 * two + head], apart, same)
            prob_grad = contract_last(keep(given), values)
            score = probs * (prob_grad - jnp.sum(probs * prob_grad, -1, keepdims=True))
            score = score.astype(LOW)
            made.append(
                (
                    dot(score, keys) * 0.125,
                    contract_first(score, query) * 0.125,
                    contract_first(probs.astype(LOW), given),
                )
            )
        for spot, one, other in zip(spots, *made):
            both = jnp.where(first, one, other)
            mixed_grad[:, spot] = both.astype(LOW)
            mixed_t[spot, :] = both.T.astype(LOW)


def unmix_kernel(
    where, mixed_grad, mix_near, mix_far, merged, residual_grad, near_v, far_v,
    merged_low, merged_t, gain_grad, bias_grad, first_grad,
):
    section = where[0]
    part(first_grad, section, False)[...] = contract_last(mixed_grad[...], mix_near[...])
    part(first_grad, section, True)[...] = contract_last(mixed_grad[...], mix_far[...])
    grad = first_grad[...]
    xhat, scale = nrm_stats(merged[...])
    gain_grad[...] = jnp.sum(grad * xhat, axis=0, keepdims=True)
    bias_grad[...] = jnp.sum(grad, axis=0, keepdims=True)
    gain = vector(section, near_v, far_v, 0, merged.shape[1] // 2)
    total = residual_grad[...] + nrm_back(xhat, scale, grad, gain)
    merged_low[...] = total.astype(LOW)
    merged_t[...] = total.T.astype(LOW)


def unmerge_kernel(where, merged_low, near_w, far_w, input_grad, skip_grad):
    near = contract_last(merged_low[...], near_w[...]).astype(LOW)
    far = contract_last(merged_low[...], far_w[...]).astype(LOW)
    input_grad[...] = jnp.where(where[0] == 0, near, far)
    skip_grad[...] = jnp.where(where[0] == 0, far, near)


def shaped(shape, kind):
    return jax.ShapeDtypeStruct(shape, kind)


def plain_call(kernel, made, operands, scratch=(), scalars=0):
    cost = sum(x.size * x.dtype.itemsize for x in operands)
    specs = [pl.BlockSpec(memory_space=pltpu.SMEM)] * scalars
    specs += [pl.BlockSpec(memory_space=pltpu.VMEM)] * (len(operands) - scalars)
    return pl.pallas_call(
        kernel,
        out_shape=made,
        in_specs=specs,
        out_specs=[pl.BlockSpec(memory_space=pltpu.VMEM)] * len(made),
        scratch_shapes=list(scratch),
        compiler_params=pltpu.CompilerParams(vmem_limit_bytes=56 << 20),
        cost_estimate=pl.CostEstimate(
            flops=128 * cost, bytes_accessed=cost, transcendentals=0
        ),
    )(*operands)


def feed_call(where, pack_near, pack_far, top, residual, near_v, far_v, up_near, up_far, down_near, down_far):
    rows, width = top.shape
    hidden = up_near.shape[1]
    steps = 8
    tile, last = hidden // steps, steps // 2 - 1
    half = width // 2

    def whole(*shape):
        return pl.BlockSpec(shape, lambda j, w: (0,) * len(shape))

    def spot(j, w):
        return (j // (steps // 2) + w[0]) % 2 * (steps // 2) + j % (steps // 2)

    def near(j):
        return jnp.minimum(j, last)

    def far(j):
        return jnp.maximum(j - last - 1, 0)

    in_specs = [
        whole(rows, width), whole(rows, width), whole(rows, width), whole(rows, width),
        whole(*near_v.shape), whole(*far_v.shape),
        pl.BlockSpec((half, tile), lambda j, w: (0, spot(j, w))),
        pl.BlockSpec((half, tile), lambda j, w: (0, spot(j, w))),
        pl.BlockSpec((tile, width), lambda j, w: (near(j), 0)),
        pl.BlockSpec((tile, width), lambda j, w: (far(j), 0)),
    ]
    out_specs = [
        pl.BlockSpec((rows, tile), lambda j, w: (0, near(j))),
        pl.BlockSpec((rows, tile), lambda j, w: (0, far(j))),
        pl.BlockSpec((tile, rows), lambda j, w: (spot(j, w), 0)),
        pl.BlockSpec((1, tile), lambda j, w: (0, spot(j, w))),
        whole(rows, width), whole(rows, width), whole(rows, width), whole(width, rows),
        whole(1, width), whole(1, width),
    ]
    made = [
        shaped((rows, hidden // 2), LOW), shaped((rows, hidden // 2), LOW),
        shaped((hidden, rows), LOW), shaped((1, hidden), FULL),
        shaped((rows, width), LOW), shaped((rows, width), FULL), shaped((rows, width), LOW),
        shaped((width, rows), LOW), shaped((1, width), FULL), shaped((1, width), FULL),
    ]
    weights = 4 * width * hidden
    return pl.pallas_call(
        feed_kernel,
        out_shape=made,
        grid_spec=pltpu.PrefetchScalarGridSpec(
            num_scalar_prefetch=1,
            grid=(steps,),
            in_specs=in_specs,
            out_specs=out_specs,
            scratch_shapes=[pltpu.VMEM((rows, width), FULL)] * 2,
        ),
        compiler_params=pltpu.CompilerParams(
            dimension_semantics=("arbitrary",), vmem_limit_bytes=56 << 20
        ),
        cost_estimate=pl.CostEstimate(
            flops=4 * rows * weights, bytes_accessed=weights, transcendentals=rows * hidden
        ),
        name="feed",
    )(where, pack_near, pack_far, top, residual, near_v, far_v, up_near, up_far, down_near, down_far)


def pick(value, spot, axis=0):
    return lax.dynamic_index_in_dim(value, spot, axis, keepdims=False)


def gather_left(torus, axes, own, far):
    chip = jnp.concatenate([own, far], axis=0)
    lead = torus.order(axes)[0]
    return jnp.concatenate([chip, torus.flip(chip, lead)], axis=0)


def gather_right(torus, axis, own):
    lead, rest = torus.order(axis)
    columns, tokens = own.shape
    split = own.reshape(*(2,) * torus.power, columns // torus.count, tokens)
    place = [torus.power - 1 - bit for bit in (lead, *rest)]
    split = split.transpose(*place, torus.power, torus.power + 1)
    split = split.reshape(2, columns // 2, tokens)
    here = torus.bit(lead)
    near = jnp.stack([pick(split, here), torus.flip(pick(split, 1 - here), lead)])
    far = pair(near)
    return jnp.concatenate([near[0], far[0], near[1], far[1]], axis=1)


def reduce_grad(torus, axis, left, right):
    rest = torus.order(axis)[1]
    halves = right.reshape(2, -1, right.shape[1])
    here = torus.bit(rest[0])
    sent = dot(pick(halves, 1 - here), left).astype(LOW)
    sent = torus.flip(sent, rest[0])
    total = dot(pick(halves, here), left) + sent.astype(FULL)
    for bit in rest[1:]:
        here = torus.bit(bit)
        held = total.astype(LOW).reshape(2, -1, left.shape[1])
        sent = torus.flip(pick(held, 1 - here), bit)
        total = pick(held, here).astype(FULL) + sent.astype(FULL)
    return total


def body(
    layer_input,
    skip_input,
    segment_ids,
    out_cotangent,
    merger,
    mixing,
    readout,
    expand,
    narrow,
    first_gain,
    first_bias,
    second_gain,
    second_bias,
    up_bias,
):
    torus = Torus(lax.axis_size("dp"))
    section = lax.axis_index("section")
    rows, width = layer_input.shape
    first_core = section == 0

    def packed(parts):
        bounds, total = [], 0
        for item in parts:
            bounds.append((total, total + item.shape[0]))
            total += item.shape[0]
        placed = [jnp.pad(item, (low, total - high)) for item, (low, high) in zip(parts, bounds)]
        return sum(placed[1:], placed[0]), bounds

    def mine(value):
        half = value.shape[-1] // 2
        return lax.dynamic_slice_in_dim(value, section * half, half, value.ndim - 1)

    merger_far = pair(merger)
    near_v, _ = packed((first_gain, first_bias, second_gain, second_bias, up_bias))
    near_v = near_v[None]
    far_v = pair(near_v)
    mixing_far = pair(mixing)
    readout_far = pair(readout)
    expand_far = pair(expand)
    narrow_far = pair(narrow)
    top_low = pair(out_cotangent)

    where = section.astype(jnp.int32).reshape(1)
    frames_mine = jnp.where(first_core, layer_input, skip_input)
    frames_other = jnp.where(first_core, skip_input, layer_input)
    segments = pick(segment_ids[0], section)[None]
    flat, tall, thin = (rows, width), (width, rows), (rows, width // 2)
    line = shaped((1, width), FULL)

    merged, low_near, low_far = plain_call(
        merge_kernel, [shaped(flat, FULL), shaped(thin, LOW), shaped(thin, LOW)],
        (where, layer_input, skip_input, merger, merger_far, near_v, far_v), scalars=1,
    )
    mixed, pack_near, pack_far, residual = plain_call(
        attend_kernel,
        [shaped((rows, 3 * width), LOW), shaped(flat, LOW), shaped(flat, LOW), shaped(flat, FULL)],
        (where, low_near, low_far, merged, segments, mixing, mixing_far, readout, readout_far,
         near_v, far_v),
        scratch=[pltpu.VMEM(flat, LOW)], scalars=1,
    )
    (act_near, act_far, lifted_t, up_bias_grad, output, residual_grad, residual_low, residual_t,
     second_gain_grad, second_bias_grad) = feed_call(
        where, pack_near, pack_far, top_low, residual, near_v, far_v, expand, expand_far, narrow,
        narrow_far,
    )
    block_output = pair(output)
    mixed_grad, mixed_t = plain_call(
        unattend_kernel,
        [shaped((rows, 3 * width), LOW), shaped((3 * width, rows), LOW)],
        (where, mixed, residual_low, segments, readout, readout_far),
        scratch=[pltpu.VMEM(flat, LOW)], scalars=1,
    )
    merged_low, merged_t, first_gain_grad, first_bias_grad = plain_call(
        unmix_kernel, [shaped(flat, LOW), shaped(tall, LOW), line, line],
        (where, mixed_grad, mixing, mixing_far, merged, residual_grad, near_v, far_v),
        scratch=[pltpu.VMEM(flat, FULL)], scalars=1,
    )
    input_grad, skip_grad = plain_call(
        unmerge_kernel, [shaped(flat, LOW)] * 2,
        (where, merged_low, merger, merger_far), scalars=1,
    )

    def left_of(axes, near, far):
        return gather_left(torus, axes, near, pair(far))

    def grad_of(axes, left, right_t):
        return reduce_grad(torus, axes, left, gather_right(torus, axes, right_t))

    half = width // 2
    merger_left = left_of("zyx", frames_mine, frames_other)
    mixing_left = left_of("zxy", low_near, low_far)
    mid_left = left_of("yxz", pack_near, pack_far)
    narrow_left = left_of("xyz", act_near, act_far)
    narrow_grad = grad_of("xyz", narrow_left, top_low.T)
    expand_grad = grad_of("yxz", mid_left[:, half:], lifted_t)
    readout_grad = grad_of("yzx", mid_left[:, :half], residual_t)
    mixing_grad = grad_of("zxy", mixing_left, mixed_t)
    merger_grad = grad_of("zyx", merger_left, merged_t)

    small, bounds = packed(
        [
            item[0]
            for item in (
                first_gain_grad, first_bias_grad, second_gain_grad, second_bias_grad, up_bias_grad
            )
        ]
    )
    small = small.reshape(-1, 128)
    small = small + pair(small)
    for bit in torus.bits["z"] + torus.bits["x"] + torus.bits["y"]:
        small = small + torus.flip(small, bit)
    small = small.reshape(-1)
    matrices = tuple(
        grad.T for grad in (merger_grad, mixing_grad, readout_grad, expand_grad, narrow_grad)
    )
    return (block_output, input_grad, skip_grad) + matrices + tuple(
        mine(small[low:high]) for low, high in bounds
    )


def solution(mesh):
    tokens = P(("section", "dp"), None)
    matrix, vector = P("section", None), P("section")
    placed = (tokens, tokens, P("dp", None, None), tokens) + (matrix,) * 5 + (vector,) * 5
    made = (tokens,) * 3 + (P("section", "dp"),) * 5 + (vector,) * 5
    return jax.shard_map(body, mesh=mesh, in_specs=placed, out_specs=made, check_vma=False)
```

```python
import jax
import jax.numpy as jnp
from jax import lax
from jax.experimental import pallas as pl
from jax.experimental.pallas import tpu as pltpu
from jax.sharding import PartitionSpec as P


HEAD_DIM = 64
LOW = jnp.bfloat16
FULL = jnp.float32


class Torus:
    def __init__(self, count):
        power = count.bit_length() - 1
        side = power // 3
        self.count, self.power = count, power
        self.bits = {
            "x": list(range(side)),
            "y": list(range(side, 2 * side)),
            "z": list(range(2 * side, power)),
        }

    def order(self, axes):
        lead = self.bits[axes[0].lower()]
        if axes[0].isupper():
            lead = lead[::-1]
        return lead[0], self.bits[axes[1]] + self.bits[axes[2]] + lead[1:]

    def bit(self, bit):
        return (lax.axis_index("dp") >> bit) & 1

    def flip(self, value, bit):
        pairs = [(source, source ^ (1 << bit)) for source in range(self.count)]
        return lax.ppermute(value, "dp", pairs)


def pair(value):
    return lax.ppermute(value, "section", [(0, 1), (1, 0)])


def dot(left, right):
    return jnp.dot(left, right, preferred_element_type=FULL)


def contract_first(left, right):
    return lax.dot_general(left, right, (((0,), (0,)), ((), ())), preferred_element_type=FULL)


def contract_last(left, right):
    return lax.dot_general(left, right, (((1,), (1,)), ((), ())), preferred_element_type=FULL)


def nrm_stats(values):
    center = values - jnp.mean(values, -1, keepdims=True)
    scale = lax.rsqrt(jnp.mean(center * center, -1, keepdims=True) + 1e-05)
    return center * scale, scale


def nrm_back(xhat, scale, grad, gain):
    g = grad * gain
    inner = g - jnp.mean(g, -1, keepdims=True) - xhat * jnp.mean(g * xhat, -1, keepdims=True)
    return scale * inner


def part(ref, section, far):
    half = ref.shape[1] // 2
    spot = (1 - section) if far else section
    return ref.at[:, pl.ds(pl.multiple_of(spot * half, half), half)]


def vector(section, near, far, low, size):
    one, two = near[:, low : low + size].astype(FULL), far[:, low : low + size].astype(FULL)
    return jnp.where(
        section == 0, jnp.concatenate([one, two], axis=1), jnp.concatenate([two, one], axis=1)
    )


def halves(section, values, near, far):
    half = values.shape[1] // 2
    one, two = values[:, :half], values[:, half:]
    near[...] = jnp.where(section == 0, one, two)
    far[...] = jnp.where(section == 0, two, one)


def merge_kernel(
    where, first_x, second_x, near_w, far_w, near_v, far_v, merged, low_near, low_far
):
    half = first_x.shape[1] // 2
    near_x = jnp.where(where[0] == 0, first_x[...], second_x[...])
    far_x = jnp.where(where[0] == 0, second_x[...], first_x[...])
    gain = vector(where[0], near_v, far_v, 0, half)
    bias = vector(where[0], near_v, far_v, half, half)
    total = dot(near_x, near_w[...]) + dot(far_x, far_w[...])
    merged[...] = total
    xhat, _ = nrm_stats(total)
    halves(where[0], (xhat * gain + bias).astype(LOW), low_near, low_far)


def score_parts(heads, segments):
    rows = segments.shape[1]
    spread = jnp.broadcast_to(segments.astype(FULL), (rows, rows))
    same = spread == spread.T
    spots = [lax.broadcasted_iota(jnp.int32, (rows, rows), axis) for axis in (0, 1)]
    apart = jnp.abs(spots[0] - spots[1]).astype(FULL)
    slopes = [2.0 ** (-8.0 * (head + 1) / heads) for head in range(heads)]
    lane = lax.broadcasted_iota(jnp.int32, (rows, 2 * HEAD_DIM), 1)
    return same, apart, slopes, lane < HEAD_DIM


def probs_of(query, keys, slope, apart, same):
    raw = contract_last(query, keys) * 0.125 - slope * apart
    raw = jnp.where(same, raw, -1000000000.0)
    raised = jnp.exp(raw - jnp.max(raw, -1, keepdims=True))
    return raised / jnp.sum(raised, -1, keepdims=True)


def attend_kernel(
    where, near_low, far_low, merged, segments, mix_near, mix_far, read_near, read_far, near_v, far_v,
    mixed, pack_near, pack_far, residual, attended,
):
    section = where[0]
    width = merged.shape[1]
    heads = width // HEAD_DIM
    near, far = near_low[...], far_low[...]
    step = width // 2
    for base in range(0, 3 * width, step):
        block = dot(near, mix_near[:, base : base + step]) + dot(far, mix_far[:, base : base + step])
        mixed[:, base : base + step] = block.astype(LOW)
    same, apart, slopes, first = score_parts(heads, segments[...])
    for two in range(heads // 2):
        lanes = slice(two * 128, two * 128 + 128)
        query = mixed[:, lanes]
        keys = mixed[:, width + two * 128 : width + two * 128 + 128]
        values = mixed[:, 2 * width + two * 128 : 2 * width + two * 128 + 128]
        blank = jnp.zeros_like(query)
        outs = []
        for head in (0, 1):
            own = jnp.where(first, query, blank) if head == 0 else jnp.where(first, blank, query)
            probs = probs_of(own, keys, slopes[2 * two + head], apart, same)
            outs.append(dot(probs.astype(LOW), values))
        attended[:, lanes] = jnp.where(first, outs[0], outs[1]).astype(LOW)
    half = width // 2
    halves(section, attended[...], pack_near.at[:, :half], pack_far.at[:, :half])
    total = merged[...] + dot(pack_near[:, :half], read_near[...])
    total = total + dot(pack_far[:, :half], read_far[...])
    residual[...] = total
    xhat, _ = nrm_stats(total)
    gain = vector(section, near_v, far_v, width, width // 2)
    bias = vector(section, near_v, far_v, width + width // 2, width // 2)
    second = (xhat * gain + bias).astype(LOW)
    halves(section, second, pack_near.at[:, half:], pack_far.at[:, half:])


def feed_kernel(
    where, pack_near, pack_far, top, residual, near_v, far_v, up_near, up_far, down_near, down_far,
    act_near, act_far, lifted_t, up_bias_grad, output, residual_grad, residual_low, residual_t,
    gain_grad, bias_grad, out_sum, grad_sum,
):
    section = where[0]
    step, steps = pl.program_id(0), pl.num_programs(0)

    @pl.when(step == 0)
    def _():
        out_sum[...] = jnp.zeros_like(out_sum)
        grad_sum[...] = jnp.zeros_like(grad_sum)

    def run(down, act, packed):
        tile = up_near.shape[1]
        spot = pl.multiple_of(2 * top.shape[1] + step % (steps // 2) * tile, tile)
        up_bias = packed[:, pl.ds(spot, tile)].astype(FULL)
        half = pack_near.shape[1] // 2
        lifted = dot(pack_near[:, half:], up_near[...])
        lifted = lifted + dot(pack_far[:, half:], up_far[...]) + up_bias
        square = lifted * lifted
        turn = jnp.tanh(0.7978845608028654 * lifted * (1.0 + 0.044715 * square))
        rise = 0.5 * (1.0 + turn)
        slope = rise + (0.5 * 0.7978845608028654) * lifted * (1.0 - turn * turn) * (
            1.0 + 3 * 0.044715 * square
        )
        active = (lifted * rise).astype(LOW)
        act[...] = active
        out_sum[...] += dot(active, down[...])
        lifted_grad = (contract_last(top[...], down[...]) * slope).astype(LOW)
        wide = lifted_grad.astype(FULL)
        up_bias_grad[...] = jnp.sum(wide, axis=0, keepdims=True)
        lifted_t[...] = wide.T.astype(LOW)
        part(grad_sum, section, False)[...] += contract_last(lifted_grad, up_near[...])
        part(grad_sum, section, True)[...] += contract_last(lifted_grad, up_far[...])

    @pl.when(step < steps // 2)
    def _():
        run(down_near, act_near, near_v)

    @pl.when(step >= steps // 2)
    def _():
        run(down_far, act_far, far_v)

    @pl.when(step == steps - 1)
    def _():
        before = residual[...]
        output[...] = (before + out_sum[...]).astype(LOW)
        grad = grad_sum[...]
        xhat, scale = nrm_stats(before)
        gain_grad[...] = jnp.sum(grad * xhat, axis=0, keepdims=True)
        bias_grad[...] = jnp.sum(grad, axis=0, keepdims=True)
        width = top.shape[1]
        gain = vector(section, near_v, far_v, width, width // 2)
        total = top[...].astype(FULL) + nrm_back(xhat, scale, grad, gain)
        residual_grad[...] = total
        residual_low[...] = total.astype(LOW)
        residual_t[...] = total.T.astype(LOW)


def unattend_kernel(
    where, mixed, residual_low, segments, read_near, read_far,
    mixed_grad, mixed_t, pulled,
):
    section = where[0]
    width = residual_low.shape[1]
    heads = width // HEAD_DIM
    grad = residual_low[...]
    part(pulled, section, False)[...] = contract_last(grad, read_near[...]).astype(LOW)
    part(pulled, section, True)[...] = contract_last(grad, read_far[...]).astype(LOW)
    same, apart, slopes, first = score_parts(heads, segments[...])
    for two in range(heads // 2):
        spots = [slice(k * width + two * 128, k * width + two * 128 + 128) for k in range(3)]
        query, keys, values = (mixed[:, spot] for spot in spots)
        given = pulled[:, spots[0]]
        blank = jnp.zeros_like(query)
        made = []
        for head in (0, 1):
            keep = (lambda v: jnp.where(first, v, blank)) if head == 0 else (
                lambda v: jnp.where(first, blank, v)
            )
            probs = probs_of(keep(query), keys, slopes[2 * two + head], apart, same)
            prob_grad = contract_last(keep(given), values)
            score = probs * (prob_grad - jnp.sum(probs * prob_grad, -1, keepdims=True))
            score = score.astype(LOW)
            made.append(
                (
                    dot(score, keys) * 0.125,
                    contract_first(score, query) * 0.125,
                    contract_first(probs.astype(LOW), given),
                )
            )
        for spot, one, other in zip(spots, *made):
            both = jnp.where(first, one, other)
            mixed_grad[:, spot] = both.astype(LOW)
            mixed_t[spot, :] = both.T.astype(LOW)


def unmix_kernel(
    where, mixed_grad, mix_near, mix_far, merged, residual_grad, near_v, far_v,
    merged_low, merged_t, gain_grad, bias_grad, first_grad,
):
    section = where[0]
    part(first_grad, section, False)[...] = contract_last(mixed_grad[...], mix_near[...])
    part(first_grad, section, True)[...] = contract_last(mixed_grad[...], mix_far[...])
    grad = first_grad[...]
    xhat, scale = nrm_stats(merged[...])
    gain_grad[...] = jnp.sum(grad * xhat, axis=0, keepdims=True)
    bias_grad[...] = jnp.sum(grad, axis=0, keepdims=True)
    gain = vector(section, near_v, far_v, 0, merged.shape[1] // 2)
    total = residual_grad[...] + nrm_back(xhat, scale, grad, gain)
    merged_low[...] = total.astype(LOW)
    merged_t[...] = total.T.astype(LOW)


def unmerge_kernel(where, merged_low, near_w, far_w, input_grad, skip_grad):
    near = contract_last(merged_low[...], near_w[...]).astype(LOW)
    far = contract_last(merged_low[...], far_w[...]).astype(LOW)
    input_grad[...] = jnp.where(where[0] == 0, near, far)
    skip_grad[...] = jnp.where(where[0] == 0, far, near)


def shaped(shape, kind):
    return jax.ShapeDtypeStruct(shape, kind)


def plain_call(kernel, made, operands, grant, scratch=(), scalars=0):
    cost = sum(x.size * x.dtype.itemsize for x in operands)
    specs = [pl.BlockSpec(memory_space=pltpu.SMEM)] * scalars
    specs += [pl.BlockSpec(memory_space=pltpu.VMEM)] * (len(operands) - scalars)
    return pl.pallas_call(
        kernel,
        out_shape=made,
        in_specs=specs,
        out_specs=[pl.BlockSpec(memory_space=pltpu.VMEM)] * len(made),
        scratch_shapes=list(scratch),
        compiler_params=pltpu.CompilerParams(vmem_limit_bytes=grant << 20),
        cost_estimate=pl.CostEstimate(
            flops=128 * cost, bytes_accessed=cost, transcendentals=0
        ),
    )(*operands)


def feed_call(where, pack_near, pack_far, top, residual, near_v, far_v, up_near, up_far, down_near, down_far):
    rows, width = top.shape
    hidden = up_near.shape[1]
    steps = 8
    tile, last = hidden // steps, steps // 2 - 1
    half = width // 2

    def whole(*shape):
        return pl.BlockSpec(shape, lambda j, w: (0,) * len(shape))

    def spot(j, w):
        return (j // (steps // 2) + w[0]) % 2 * (steps // 2) + j % (steps // 2)

    def near(j):
        return jnp.minimum(j, last)

    def far(j):
        return jnp.maximum(j - last - 1, 0)

    in_specs = [
        whole(rows, width), whole(rows, width), whole(rows, width), whole(rows, width),
        whole(*near_v.shape), whole(*far_v.shape),
        pl.BlockSpec((half, tile), lambda j, w: (0, spot(j, w))),
        pl.BlockSpec((half, tile), lambda j, w: (0, spot(j, w))),
        pl.BlockSpec((tile, width), lambda j, w: (near(j), 0)),
        pl.BlockSpec((tile, width), lambda j, w: (far(j), 0)),
    ]
    out_specs = [
        pl.BlockSpec((rows, tile), lambda j, w: (0, near(j))),
        pl.BlockSpec((rows, tile), lambda j, w: (0, far(j))),
        pl.BlockSpec((tile, rows), lambda j, w: (spot(j, w), 0)),
        pl.BlockSpec((1, tile), lambda j, w: (0, spot(j, w))),
        whole(rows, width), whole(rows, width), whole(rows, width), whole(width, rows),
        whole(1, width), whole(1, width),
    ]
    made = [
        shaped((rows, hidden // 2), LOW), shaped((rows, hidden // 2), LOW),
        shaped((hidden, rows), LOW), shaped((1, hidden), FULL),
        shaped((rows, width), LOW), shaped((rows, width), FULL), shaped((rows, width), LOW),
        shaped((width, rows), LOW), shaped((1, width), FULL), shaped((1, width), FULL),
    ]
    weights = 4 * width * hidden
    return pl.pallas_call(
        feed_kernel,
        out_shape=made,
        grid_spec=pltpu.PrefetchScalarGridSpec(
            num_scalar_prefetch=1,
            grid=(steps,),
            in_specs=in_specs,
            out_specs=out_specs,
            scratch_shapes=[pltpu.VMEM((rows, width), FULL)] * 2,
        ),
        compiler_params=pltpu.CompilerParams(
            dimension_semantics=("arbitrary",), vmem_limit_bytes=24 << 20
        ),
        cost_estimate=pl.CostEstimate(
            flops=4 * rows * weights, bytes_accessed=weights, transcendentals=rows * hidden
        ),
        name="feed",
    )(where, pack_near, pack_far, top, residual, near_v, far_v, up_near, up_far, down_near, down_far)


def pick(value, spot, axis=0):
    return lax.dynamic_index_in_dim(value, spot, axis, keepdims=False)


def gather_left(torus, axes, own, far):
    chip = jnp.concatenate([own, far], axis=0)
    lead = torus.order(axes)[0]
    return jnp.concatenate([chip, torus.flip(chip, lead)], axis=0)


def gather_right(torus, axis, own):
    lead, rest = torus.order(axis)
    columns, tokens = own.shape
    split = own.reshape(*(2,) * torus.power, columns // torus.count, tokens)
    place = [torus.power - 1 - bit for bit in (lead, *rest)]
    split = split.transpose(*place, torus.power, torus.power + 1)
    split = split.reshape(2, columns // 2, tokens)
    here = torus.bit(lead)
    near = jnp.stack([pick(split, here), torus.flip(pick(split, 1 - here), lead)])
    far = pair(near)
    return jnp.concatenate([near[0], far[0], near[1], far[1]], axis=1)


def reduce_grad(torus, axis, left, right):
    rest = torus.order(axis)[1]
    halves = right.reshape(2, -1, right.shape[1])
    here = torus.bit(rest[0])
    sent = dot(pick(halves, 1 - here), left).astype(LOW)
    sent = torus.flip(sent, rest[0])
    total = dot(pick(halves, here), left) + sent.astype(FULL)
    for bit in rest[1:]:
        here = torus.bit(bit)
        held = total.astype(LOW).reshape(2, -1, left.shape[1])
        sent = torus.flip(pick(held, 1 - here), bit)
        total = pick(held, here).astype(FULL) + sent.astype(FULL)
    return total


def body(
    layer_input,
    skip_input,
    segment_ids,
    out_cotangent,
    merger,
    mixing,
    readout,
    expand,
    narrow,
    first_gain,
    first_bias,
    second_gain,
    second_bias,
    up_bias,
):
    torus = Torus(lax.axis_size("dp"))
    section = lax.axis_index("section")
    rows, width = layer_input.shape
    first_core = section == 0

    def packed(parts):
        bounds, total = [], 0
        for item in parts:
            bounds.append((total, total + item.shape[0]))
            total += item.shape[0]
        placed = [jnp.pad(item, (low, total - high)) for item, (low, high) in zip(parts, bounds)]
        return sum(placed[1:], placed[0]), bounds

    def mine(value):
        half = value.shape[-1] // 2
        return lax.dynamic_slice_in_dim(value, section * half, half, value.ndim - 1)

    merger_far = pair(merger)
    near_v, _ = packed((first_gain, first_bias, second_gain, second_bias, up_bias))
    near_v = near_v[None]
    far_v = pair(near_v)
    mixing_far = pair(mixing)
    readout_far = pair(readout)
    expand_far = pair(expand)
    narrow_far = pair(narrow)
    top_low = pair(out_cotangent)

    where = section.astype(jnp.int32).reshape(1)
    frames_mine = jnp.where(first_core, layer_input, skip_input)
    frames_other = jnp.where(first_core, skip_input, layer_input)
    segments = pick(segment_ids[0], section)[None]
    flat, tall, thin = (rows, width), (width, rows), (rows, width // 2)
    line = shaped((1, width), FULL)

    merged, low_near, low_far = plain_call(
        merge_kernel, [shaped(flat, FULL), shaped(thin, LOW), shaped(thin, LOW)],
        (where, layer_input, skip_input, merger, merger_far, near_v, far_v), 12, scalars=1,
    )
    mixed, pack_near, pack_far, residual = plain_call(
        attend_kernel,
        [shaped((rows, 3 * width), LOW), shaped(flat, LOW), shaped(flat, LOW), shaped(flat, FULL)],
        (where, low_near, low_far, merged, segments, mixing, mixing_far, readout, readout_far,
         near_v, far_v),
        24, scratch=[pltpu.VMEM(flat, LOW)], scalars=1,
    )
    (act_near, act_far, lifted_t, up_bias_grad, output, residual_grad, residual_low, residual_t,
     second_gain_grad, second_bias_grad) = feed_call(
        where, pack_near, pack_far, top_low, residual, near_v, far_v, expand, expand_far, narrow,
        narrow_far,
    )
    block_output = pair(output)
    mixed_grad, mixed_t = plain_call(
        unattend_kernel,
        [shaped((rows, 3 * width), LOW), shaped((3 * width, rows), LOW)],
        (where, mixed, residual_low, segments, readout, readout_far),
        16, scratch=[pltpu.VMEM(flat, LOW)], scalars=1,
    )
    merged_low, merged_t, first_gain_grad, first_bias_grad = plain_call(
        unmix_kernel, [shaped(flat, LOW), shaped(tall, LOW), line, line],
        (where, mixed_grad, mixing, mixing_far, merged, residual_grad, near_v, far_v),
        16, scratch=[pltpu.VMEM(flat, FULL)], scalars=1,
    )
    input_grad, skip_grad = plain_call(
        unmerge_kernel, [shaped(flat, LOW)] * 2,
        (where, merged_low, merger, merger_far), 12, scalars=1,
    )

    def left_of(axes, near, far):
        return gather_left(torus, axes, near, pair(far))

    def grad_of(axes, left, right_t):
        return reduce_grad(torus, axes, left, gather_right(torus, axes, right_t))

    half = width // 2
    merger_left = left_of("zyx", frames_mine, frames_other)
    mixing_left = left_of("Zxy", low_near, low_far)
    mid_left = left_of("yxz", pack_near, pack_far)
    narrow_left = left_of("xyz", act_near, act_far)
    narrow_grad = grad_of("xyz", narrow_left, top_low.T)
    expand_grad = grad_of("yxz", mid_left[:, half:], lifted_t)
    readout_grad = grad_of("yzx", mid_left[:, :half], residual_t)
    mixing_grad = grad_of("Zxy", mixing_left, mixed_t)
    merger_grad = grad_of("zyx", merger_left, merged_t)

    small, bounds = packed(
        [
            item[0]
            for item in (
                first_gain_grad, first_bias_grad, second_gain_grad, second_bias_grad, up_bias_grad
            )
        ]
    )
    small = small.reshape(-1, 128)
    small = small + pair(small)
    for bit in torus.bits["z"] + torus.bits["x"] + torus.bits["y"]:
        small = small + torus.flip(small, bit)
    small = small.reshape(-1)
    matrices = tuple(
        grad.T for grad in (merger_grad, mixing_grad, readout_grad, expand_grad, narrow_grad)
    )
    return (block_output, input_grad, skip_grad) + matrices + tuple(
        mine(small[low:high]) for low, high in bounds
    )


def solution(mesh):
    tokens = P(("section", "dp"), None)
    matrix, vector = P("section", None), P("section")
    placed = (tokens, tokens, P("dp", None, None), tokens) + (matrix,) * 5 + (vector,) * 5
    made = (tokens,) * 3 + (P("section", "dp"),) * 5 + (vector,) * 5
    return jax.shard_map(body, mesh=mesh, in_specs=placed, out_specs=made, check_vma=False)
```

```python
import jax
import jax.numpy as jnp
from jax import lax
from jax.experimental import pallas as pl
from jax.experimental.pallas import tpu as pltpu
from jax.sharding import PartitionSpec as P


HEAD_DIM = 64
LOW = jnp.bfloat16
FULL = jnp.float32


class Torus:
    def __init__(self, count):
        power = count.bit_length() - 1
        side = power // 3
        self.count, self.power = count, power
        self.bits = {
            "x": list(range(side)),
            "y": list(range(side, 2 * side)),
            "z": list(range(2 * side, power)),
        }

    def order(self, axes):
        lead = self.bits[axes[0].lower()]
        if axes[0].isupper():
            lead = lead[::-1]
        return lead[0], self.bits[axes[1]] + self.bits[axes[2]] + lead[1:]

    def bit(self, bit):
        return (lax.axis_index("dp") >> bit) & 1

    def flip(self, value, bit):
        pairs = [(source, source ^ (1 << bit)) for source in range(self.count)]
        return lax.ppermute(value, "dp", pairs)


def pair(value):
    return lax.ppermute(value, "section", [(0, 1), (1, 0)])


def dot(left, right):
    return jnp.dot(left, right, preferred_element_type=FULL)


def contract_first(left, right):
    return lax.dot_general(left, right, (((0,), (0,)), ((), ())), preferred_element_type=FULL)


def contract_last(left, right):
    return lax.dot_general(left, right, (((1,), (1,)), ((), ())), preferred_element_type=FULL)


def nrm_stats(values):
    center = values - jnp.mean(values, -1, keepdims=True)
    scale = lax.rsqrt(jnp.mean(center * center, -1, keepdims=True) + 1e-05)
    return center * scale, scale


def nrm_back(xhat, scale, grad, gain):
    g = grad * gain
    inner = g - jnp.mean(g, -1, keepdims=True) - xhat * jnp.mean(g * xhat, -1, keepdims=True)
    return scale * inner


def part(ref, section, far):
    half = ref.shape[1] // 2
    spot = (1 - section) if far else section
    return ref.at[:, pl.ds(pl.multiple_of(spot * half, half), half)]


def vector(section, near, far, low, size):
    one, two = near[:, low : low + size].astype(FULL), far[:, low : low + size].astype(FULL)
    return jnp.where(
        section == 0, jnp.concatenate([one, two], axis=1), jnp.concatenate([two, one], axis=1)
    )


def halves(section, values, near, far):
    half = values.shape[1] // 2
    one, two = values[:, :half], values[:, half:]
    near[...] = jnp.where(section == 0, one, two)
    far[...] = jnp.where(section == 0, two, one)


def merge_kernel(
    where, first_x, second_x, near_w, far_w, near_v, far_v, top,
    merged, low_near, low_far, top_t,
):
    half = first_x.shape[1] // 2
    near_x = jnp.where(where[0] == 0, first_x[...], second_x[...])
    far_x = jnp.where(where[0] == 0, second_x[...], first_x[...])
    gain = vector(where[0], near_v, far_v, 0, half)
    bias = vector(where[0], near_v, far_v, half, half)
    total = dot(near_x, near_w[...]) + dot(far_x, far_w[...])
    merged[...] = total
    xhat, _ = nrm_stats(total)
    halves(where[0], (xhat * gain + bias).astype(LOW), low_near, low_far)
    top_t[...] = top[...].astype(FULL).T.astype(LOW)


def score_parts(heads, segments):
    rows = segments.shape[1]
    spread = jnp.broadcast_to(segments.astype(FULL), (rows, rows))
    same = spread == spread.T
    spots = [lax.broadcasted_iota(jnp.int32, (rows, rows), axis) for axis in (0, 1)]
    apart = jnp.abs(spots[0] - spots[1]).astype(FULL)
    slopes = [2.0 ** (-8.0 * (head + 1) / heads) for head in range(heads)]
    lane = lax.broadcasted_iota(jnp.int32, (rows, 2 * HEAD_DIM), 1)
    return same, apart, slopes, lane < HEAD_DIM


def probs_of(query, keys, slope, apart, same):
    raw = contract_last(query, keys) * 0.125 - slope * apart
    raw = jnp.where(same, raw, -1000000000.0)
    raised = jnp.exp(raw - jnp.max(raw, -1, keepdims=True))
    return raised / jnp.sum(raised, -1, keepdims=True)


def attend_kernel(
    where, near_low, far_low, merged, segments, mix_near, mix_far, read_near, read_far, near_v, far_v,
    mixed, pack_near, pack_far, residual, attended,
):
    section = where[0]
    width = merged.shape[1]
    heads = width // HEAD_DIM
    near, far = near_low[...], far_low[...]
    step = width // 2
    for base in range(0, 3 * width, step):
        block = dot(near, mix_near[:, base : base + step]) + dot(far, mix_far[:, base : base + step])
        mixed[:, base : base + step] = block.astype(LOW)
    same, apart, slopes, first = score_parts(heads, segments[...])
    for two in range(heads // 2):
        lanes = slice(two * 128, two * 128 + 128)
        query = mixed[:, lanes]
        keys = mixed[:, width + two * 128 : width + two * 128 + 128]
        values = mixed[:, 2 * width + two * 128 : 2 * width + two * 128 + 128]
        blank = jnp.zeros_like(query)
        outs = []
        for head in (0, 1):
            own = jnp.where(first, query, blank) if head == 0 else jnp.where(first, blank, query)
            probs = probs_of(own, keys, slopes[2 * two + head], apart, same)
            outs.append(dot(probs.astype(LOW), values))
        attended[:, lanes] = jnp.where(first, outs[0], outs[1]).astype(LOW)
    half = width // 2
    halves(section, attended[...], pack_near.at[:, :half], pack_far.at[:, :half])
    total = merged[...] + dot(pack_near[:, :half], read_near[...])
    total = total + dot(pack_far[:, :half], read_far[...])
    residual[...] = total
    xhat, _ = nrm_stats(total)
    gain = vector(section, near_v, far_v, width, width // 2)
    bias = vector(section, near_v, far_v, width + width // 2, width // 2)
    second = (xhat * gain + bias).astype(LOW)
    halves(section, second, pack_near.at[:, half:], pack_far.at[:, half:])


def feed_kernel(
    where, pack_near, pack_far, top, residual, near_v, far_v, up_near, up_far, down_near, down_far,
    act_near, act_far, lifted_t, up_bias_grad, output, residual_grad, residual_low, residual_t,
    gain_grad, bias_grad, out_sum, grad_sum,
):
    section = where[0]
    step, steps = pl.program_id(0), pl.num_programs(0)

    @pl.when(step == 0)
    def _():
        out_sum[...] = jnp.zeros_like(out_sum)
        grad_sum[...] = jnp.zeros_like(grad_sum)

    def run(down, act, packed):
        tile = up_near.shape[1]
        spot = pl.multiple_of(2 * top.shape[1] + step % (steps // 2) * tile, tile)
        up_bias = packed[:, pl.ds(spot, tile)].astype(FULL)
        half = pack_near.shape[1] // 2
        lifted = dot(pack_near[:, half:], up_near[...])
        lifted = lifted + dot(pack_far[:, half:], up_far[...]) + up_bias
        square = lifted * lifted
        turn = jnp.tanh(0.7978845608028654 * lifted * (1.0 + 0.044715 * square))
        rise = 0.5 * (1.0 + turn)
        slope = rise + (0.5 * 0.7978845608028654) * lifted * (1.0 - turn * turn) * (
            1.0 + 3 * 0.044715 * square
        )
        active = (lifted * rise).astype(LOW)
        act[...] = active
        out_sum[...] += dot(active, down[...])
        lifted_grad = (contract_last(top[...], down[...]) * slope).astype(LOW)
        wide = lifted_grad.astype(FULL)
        up_bias_grad[...] = jnp.sum(wide, axis=0, keepdims=True)
        lifted_t[...] = wide.T.astype(LOW)
        part(grad_sum, section, False)[...] += contract_last(lifted_grad, up_near[...])
        part(grad_sum, section, True)[...] += contract_last(lifted_grad, up_far[...])

    @pl.when(step < steps // 2)
    def _():
        run(down_near, act_near, near_v)

    @pl.when(step >= steps // 2)
    def _():
        run(down_far, act_far, far_v)

    @pl.when(step == steps - 1)
    def _():
        before = residual[...]
        output[...] = (before + out_sum[...]).astype(LOW)
        grad = grad_sum[...]
        xhat, scale = nrm_stats(before)
        gain_grad[...] = jnp.sum(grad * xhat, axis=0, keepdims=True)
        bias_grad[...] = jnp.sum(grad, axis=0, keepdims=True)
        width = top.shape[1]
        gain = vector(section, near_v, far_v, width, width // 2)
        total = top[...].astype(FULL) + nrm_back(xhat, scale, grad, gain)
        residual_grad[...] = total
        residual_low[...] = total.astype(LOW)
        residual_t[...] = total.T.astype(LOW)


def unattend_kernel(
    where, mixed, residual_low, segments, read_near, read_far,
    mixed_grad, mixed_t, pulled,
):
    section = where[0]
    width = residual_low.shape[1]
    heads = width // HEAD_DIM
    grad = residual_low[...]
    part(pulled, section, False)[...] = contract_last(grad, read_near[...]).astype(LOW)
    part(pulled, section, True)[...] = contract_last(grad, read_far[...]).astype(LOW)
    same, apart, slopes, first = score_parts(heads, segments[...])
    for two in range(heads // 2):
        spots = [slice(k * width + two * 128, k * width + two * 128 + 128) for k in range(3)]
        query, keys, values = (mixed[:, spot] for spot in spots)
        given = pulled[:, spots[0]]
        blank = jnp.zeros_like(query)
        made = []
        for head in (0, 1):
            keep = (lambda v: jnp.where(first, v, blank)) if head == 0 else (
                lambda v: jnp.where(first, blank, v)
            )
            probs = probs_of(keep(query), keys, slopes[2 * two + head], apart, same)
            prob_grad = contract_last(keep(given), values)
            score = probs * (prob_grad - jnp.sum(probs * prob_grad, -1, keepdims=True))
            score = score.astype(LOW)
            made.append(
                (
                    dot(score, keys) * 0.125,
                    contract_first(score, query) * 0.125,
                    contract_first(probs.astype(LOW), given),
                )
            )
        for spot, one, other in zip(spots, *made):
            both = jnp.where(first, one, other)
            mixed_grad[:, spot] = both.astype(LOW)
            mixed_t[spot, :] = both.T.astype(LOW)


def unmix_kernel(
    where, mixed_grad, mix_near, mix_far, merged, residual_grad, near_v, far_v,
    merged_low, merged_t, gain_grad, bias_grad, first_grad,
):
    section = where[0]
    part(first_grad, section, False)[...] = contract_last(mixed_grad[...], mix_near[...])
    part(first_grad, section, True)[...] = contract_last(mixed_grad[...], mix_far[...])
    grad = first_grad[...]
    xhat, scale = nrm_stats(merged[...])
    gain_grad[...] = jnp.sum(grad * xhat, axis=0, keepdims=True)
    bias_grad[...] = jnp.sum(grad, axis=0, keepdims=True)
    gain = vector(section, near_v, far_v, 0, merged.shape[1] // 2)
    total = residual_grad[...] + nrm_back(xhat, scale, grad, gain)
    merged_low[...] = total.astype(LOW)
    merged_t[...] = total.T.astype(LOW)


def unmerge_kernel(where, merged_low, near_w, far_w, input_grad, skip_grad):
    near = contract_last(merged_low[...], near_w[...]).astype(LOW)
    far = contract_last(merged_low[...], far_w[...]).astype(LOW)
    input_grad[...] = jnp.where(where[0] == 0, near, far)
    skip_grad[...] = jnp.where(where[0] == 0, far, near)


def shaped(shape, kind):
    return jax.ShapeDtypeStruct(shape, kind)


def plain_call(kernel, made, operands, grant, scratch=(), scalars=0):
    cost = sum(x.size * x.dtype.itemsize for x in operands)
    specs = [pl.BlockSpec(memory_space=pltpu.SMEM)] * scalars
    specs += [pl.BlockSpec(memory_space=pltpu.VMEM)] * (len(operands) - scalars)
    return pl.pallas_call(
        kernel,
        out_shape=made,
        in_specs=specs,
        out_specs=[pl.BlockSpec(memory_space=pltpu.VMEM)] * len(made),
        scratch_shapes=list(scratch),
        compiler_params=pltpu.CompilerParams(vmem_limit_bytes=grant << 20),
        cost_estimate=pl.CostEstimate(
            flops=128 * cost, bytes_accessed=cost, transcendentals=0
        ),
    )(*operands)


def feed_call(where, pack_near, pack_far, top, residual, near_v, far_v, up_near, up_far, down_near, down_far):
    rows, width = top.shape
    hidden = up_near.shape[1]
    steps = 8
    tile, last = hidden // steps, steps // 2 - 1
    half = width // 2

    def whole(*shape):
        return pl.BlockSpec(shape, lambda j, w: (0,) * len(shape))

    def spot(j, w):
        return (j // (steps // 2) + w[0]) % 2 * (steps // 2) + j % (steps // 2)

    def near(j):
        return jnp.minimum(j, last)

    def far(j):
        return jnp.maximum(j - last - 1, 0)

    in_specs = [
        whole(rows, width), whole(rows, width), whole(rows, width), whole(rows, width),
        whole(*near_v.shape), whole(*far_v.shape),
        pl.BlockSpec((half, tile), lambda j, w: (0, spot(j, w))),
        pl.BlockSpec((half, tile), lambda j, w: (0, spot(j, w))),
        pl.BlockSpec((tile, width), lambda j, w: (near(j), 0)),
        pl.BlockSpec((tile, width), lambda j, w: (far(j), 0)),
    ]
    out_specs = [
        pl.BlockSpec((rows, tile), lambda j, w: (0, near(j))),
        pl.BlockSpec((rows, tile), lambda j, w: (0, far(j))),
        pl.BlockSpec((tile, rows), lambda j, w: (spot(j, w), 0)),
        pl.BlockSpec((1, tile), lambda j, w: (0, spot(j, w))),
        whole(rows, width), whole(rows, width), whole(rows, width), whole(width, rows),
        whole(1, width), whole(1, width),
    ]
    made = [
        shaped((rows, hidden // 2), LOW), shaped((rows, hidden // 2), LOW),
        shaped((hidden, rows), LOW), shaped((1, hidden), FULL),
        shaped((rows, width), LOW), shaped((rows, width), FULL), shaped((rows, width), LOW),
        shaped((width, rows), LOW), shaped((1, width), FULL), shaped((1, width), FULL),
    ]
    weights = 4 * width * hidden
    return pl.pallas_call(
        feed_kernel,
        out_shape=made,
        grid_spec=pltpu.PrefetchScalarGridSpec(
            num_scalar_prefetch=1,
            grid=(steps,),
            in_specs=in_specs,
            out_specs=out_specs,
            scratch_shapes=[pltpu.VMEM((rows, width), FULL)] * 2,
        ),
        compiler_params=pltpu.CompilerParams(
            dimension_semantics=("arbitrary",), vmem_limit_bytes=24 << 20
        ),
        cost_estimate=pl.CostEstimate(
            flops=4 * rows * weights, bytes_accessed=weights, transcendentals=rows * hidden
        ),
        name="feed",
    )(where, pack_near, pack_far, top, residual, near_v, far_v, up_near, up_far, down_near, down_far)


def pick(value, spot, axis=0):
    return lax.dynamic_index_in_dim(value, spot, axis, keepdims=False)


def gather_left(torus, axes, own, far):
    chip = jnp.concatenate([own, far], axis=0)
    lead = torus.order(axes)[0]
    return jnp.concatenate([chip, torus.flip(chip, lead)], axis=0)


def gather_right(torus, axis, own):
    lead, rest = torus.order(axis)
    columns, tokens = own.shape
    split = own.reshape(*(2,) * torus.power, columns // torus.count, tokens)
    place = [torus.power - 1 - bit for bit in (lead, *rest)]
    split = split.transpose(*place, torus.power, torus.power + 1)
    split = split.reshape(2, columns // 2, tokens)
    here = torus.bit(lead)
    near = jnp.stack([pick(split, here), torus.flip(pick(split, 1 - here), lead)])
    far = pair(near)
    return jnp.concatenate([near[0], far[0], near[1], far[1]], axis=1)


def reduce_grad(torus, axis, left, right):
    rest = torus.order(axis)[1]
    halves = right.reshape(2, -1, right.shape[1])
    here = torus.bit(rest[0])
    sent = dot(pick(halves, 1 - here), left).astype(LOW)
    sent = torus.flip(sent, rest[0])
    total = dot(pick(halves, here), left) + sent.astype(FULL)
    for bit in rest[1:]:
        here = torus.bit(bit)
        held = total.astype(LOW).reshape(2, -1, left.shape[1])
        sent = torus.flip(pick(held, 1 - here), bit)
        total = pick(held, here).astype(FULL) + sent.astype(FULL)
    return total


def body(
    layer_input,
    skip_input,
    segment_ids,
    out_cotangent,
    merger,
    mixing,
    readout,
    expand,
    narrow,
    first_gain,
    first_bias,
    second_gain,
    second_bias,
    up_bias,
):
    torus = Torus(lax.axis_size("dp"))
    section = lax.axis_index("section")
    rows, width = layer_input.shape
    first_core = section == 0

    def packed(parts):
        bounds, total = [], 0
        for item in parts:
            bounds.append((total, total + item.shape[0]))
            total += item.shape[0]
        placed = [jnp.pad(item, (low, total - high)) for item, (low, high) in zip(parts, bounds)]
        return sum(placed[1:], placed[0]), bounds

    def mine(value):
        half = value.shape[-1] // 2
        return lax.dynamic_slice_in_dim(value, section * half, half, value.ndim - 1)

    merger_far = pair(merger)
    near_v, _ = packed((first_gain, first_bias, second_gain, second_bias, up_bias))
    near_v = near_v[None]
    far_v = pair(near_v)
    mixing_far = pair(mixing)
    readout_far = pair(readout)
    expand_far = pair(expand)
    narrow_far = pair(narrow)
    top_low = pair(out_cotangent)

    where = section.astype(jnp.int32).reshape(1)
    frames_mine = jnp.where(first_core, layer_input, skip_input)
    frames_other = jnp.where(first_core, skip_input, layer_input)
    segments = pick(segment_ids[0], section)[None]
    flat, tall, thin = (rows, width), (width, rows), (rows, width // 2)
    line = shaped((1, width), FULL)

    merged, low_near, low_far, top_t = plain_call(
        merge_kernel,
        [shaped(flat, FULL), shaped(thin, LOW), shaped(thin, LOW), shaped(tall, LOW)],
        (where, layer_input, skip_input, merger, merger_far, near_v, far_v, top_low), 12, scalars=1,
    )
    mixed, pack_near, pack_far, residual = plain_call(
        attend_kernel,
        [shaped((rows, 3 * width), LOW), shaped(flat, LOW), shaped(flat, LOW), shaped(flat, FULL)],
        (where, low_near, low_far, merged, segments, mixing, mixing_far, readout, readout_far,
         near_v, far_v),
        24, scratch=[pltpu.VMEM(flat, LOW)], scalars=1,
    )
    (act_near, act_far, lifted_t, up_bias_grad, output, residual_grad, residual_low, residual_t,
     second_gain_grad, second_bias_grad) = feed_call(
        where, pack_near, pack_far, top_low, residual, near_v, far_v, expand, expand_far, narrow,
        narrow_far,
    )
    block_output = pair(output)
    mixed_grad, mixed_t = plain_call(
        unattend_kernel,
        [shaped((rows, 3 * width), LOW), shaped((3 * width, rows), LOW)],
        (where, mixed, residual_low, segments, readout, readout_far),
        16, scratch=[pltpu.VMEM(flat, LOW)], scalars=1,
    )
    merged_low, merged_t, first_gain_grad, first_bias_grad = plain_call(
        unmix_kernel, [shaped(flat, LOW), shaped(tall, LOW), line, line],
        (where, mixed_grad, mixing, mixing_far, merged, residual_grad, near_v, far_v),
        16, scratch=[pltpu.VMEM(flat, FULL)], scalars=1,
    )
    input_grad, skip_grad = plain_call(
        unmerge_kernel, [shaped(flat, LOW)] * 2,
        (where, merged_low, merger, merger_far), 12, scalars=1,
    )

    def left_of(axes, near, far):
        return gather_left(torus, axes, near, pair(far))

    def grad_of(axes, left, right_t):
        return reduce_grad(torus, axes, left, gather_right(torus, axes, right_t))

    half = width // 2
    merger_left = left_of("yzx", frames_mine, frames_other)
    mixing_left = left_of("Zxy", low_near, low_far)
    mid_left = left_of("zxy", pack_near, pack_far)
    narrow_left = left_of("xyz", act_near, act_far)
    narrow_grad = grad_of("xyz", narrow_left, top_t)
    expand_grad = grad_of("zxy", mid_left[:, half:], lifted_t)
    readout_grad = grad_of("zyx", mid_left[:, :half], residual_t)
    mixing_grad = grad_of("Zxy", mixing_left, mixed_t)
    merger_grad = grad_of("yzx", merger_left, merged_t)

    small, bounds = packed(
        [
            item[0]
            for item in (
                first_gain_grad, first_bias_grad, second_gain_grad, second_bias_grad, up_bias_grad
            )
        ]
    )
    small = small.reshape(-1, 128)
    small = small + pair(small)
    for bit in torus.bits["z"] + torus.bits["x"] + torus.bits["y"]:
        small = small + torus.flip(small, bit)
    small = small.reshape(-1)
    matrices = tuple(
        grad.T for grad in (merger_grad, mixing_grad, readout_grad, expand_grad, narrow_grad)
    )
    return (block_output, input_grad, skip_grad) + matrices + tuple(
        mine(small[low:high]) for low, high in bounds
    )


def solution(mesh):
    tokens = P(("section", "dp"), None)
    matrix, vector = P("section", None), P("section")
    placed = (tokens, tokens, P("dp", None, None), tokens) + (matrix,) * 5 + (vector,) * 5
    made = (tokens,) * 3 + (P("section", "dp"),) * 5 + (vector,) * 5
    return jax.shard_map(body, mesh=mesh, in_specs=placed, out_specs=made, check_vma=False)
```

```python
import jax
import jax.numpy as jnp
from jax import lax
from jax.experimental import pallas as pl
from jax.experimental.pallas import tpu as pltpu
from jax.sharding import PartitionSpec as P


HEAD_DIM = 64
LOW = jnp.bfloat16
FULL = jnp.float32


class Torus:
    def __init__(self, count):
        power = count.bit_length() - 1
        side = power // 3
        self.count, self.power = count, power
        self.bits = {
            "x": list(range(side)),
            "y": list(range(side, 2 * side)),
            "z": list(range(2 * side, power)),
        }

    def order(self, axes):
        lead = self.bits[axes[0].lower()]
        if axes[0].isupper():
            lead = lead[::-1]
        return lead[0], self.bits[axes[1]] + self.bits[axes[2]] + lead[1:]

    def bit(self, bit):
        return (lax.axis_index("dp") >> bit) & 1

    def flip(self, value, bit):
        pairs = [(source, source ^ (1 << bit)) for source in range(self.count)]
        return lax.ppermute(value, "dp", pairs)


def pair(value):
    return lax.ppermute(value, "section", [(0, 1), (1, 0)])


def dot(left, right):
    return jnp.dot(left, right, preferred_element_type=FULL)


def contract_first(left, right):
    return lax.dot_general(left, right, (((0,), (0,)), ((), ())), preferred_element_type=FULL)


def contract_last(left, right):
    return lax.dot_general(left, right, (((1,), (1,)), ((), ())), preferred_element_type=FULL)


def nrm_stats(values):
    center = values - jnp.mean(values, -1, keepdims=True)
    scale = lax.rsqrt(jnp.mean(center * center, -1, keepdims=True) + 1e-05)
    return center * scale, scale


def nrm_back(xhat, scale, grad, gain):
    g = grad * gain
    inner = g - jnp.mean(g, -1, keepdims=True) - xhat * jnp.mean(g * xhat, -1, keepdims=True)
    return scale * inner


def part(ref, section, far):
    half = ref.shape[1] // 2
    spot = (1 - section) if far else section
    return ref.at[:, pl.ds(pl.multiple_of(spot * half, half), half)]


def vector(section, near, far, low, size):
    one, two = near[:, low : low + size].astype(FULL), far[:, low : low + size].astype(FULL)
    return jnp.where(
        section == 0, jnp.concatenate([one, two], axis=1), jnp.concatenate([two, one], axis=1)
    )


def halves(section, values, near, far):
    half = values.shape[1] // 2
    one, two = values[:, :half], values[:, half:]
    near[...] = jnp.where(section == 0, one, two)
    far[...] = jnp.where(section == 0, two, one)


def merge_kernel(
    where, first_x, second_x, near_w, far_w, near_v, far_v, top,
    merged, low_near, low_far, top_t,
):
    half = first_x.shape[1] // 2
    near_x = jnp.where(where[0] == 0, first_x[...], second_x[...])
    far_x = jnp.where(where[0] == 0, second_x[...], first_x[...])
    gain = vector(where[0], near_v, far_v, 0, half)
    bias = vector(where[0], near_v, far_v, half, half)
    total = dot(near_x, near_w[...]) + dot(far_x, far_w[...])
    merged[...] = total
    xhat, _ = nrm_stats(total)
    halves(where[0], (xhat * gain + bias).astype(LOW), low_near, low_far)
    top_t[...] = top[...].astype(FULL).T.astype(LOW)


def score_parts(heads, segments):
    rows = segments.shape[1]
    spread = jnp.broadcast_to(segments.astype(FULL), (rows, rows))
    same = spread == spread.T
    spots = [lax.broadcasted_iota(jnp.int32, (rows, rows), axis) for axis in (0, 1)]
    apart = jnp.abs(spots[0] - spots[1]).astype(FULL)
    slopes = [2.0 ** (-8.0 * (head + 1) / heads) for head in range(heads)]
    lane = lax.broadcasted_iota(jnp.int32, (rows, 2 * HEAD_DIM), 1)
    return same, apart, slopes, lane < HEAD_DIM


def probs_of(query, keys, slope, apart, same):
    raw = contract_last(query, keys) * 0.125 - slope * apart
    raw = jnp.where(same, raw, -1000000000.0)
    raised = jnp.exp(raw - jnp.max(raw, -1, keepdims=True))
    return raised / jnp.sum(raised, -1, keepdims=True)


def attend_kernel(
    where, near_low, far_low, merged, segments, mix_near, mix_far, read_near, read_far, near_v, far_v,
    mixed, pack_near, pack_far, residual, attended,
):
    section = where[0]
    width = merged.shape[1]
    heads = width // HEAD_DIM
    near, far = near_low[...], far_low[...]
    step = width // 2
    for base in range(0, 3 * width, step):
        block = dot(near, mix_near[:, base : base + step]) + dot(far, mix_far[:, base : base + step])
        mixed[:, base : base + step] = block.astype(LOW)
    same, apart, slopes, first = score_parts(heads, segments[...])
    for two in range(heads // 2):
        lanes = slice(two * 128, two * 128 + 128)
        query = mixed[:, lanes]
        keys = mixed[:, width + two * 128 : width + two * 128 + 128]
        values = mixed[:, 2 * width + two * 128 : 2 * width + two * 128 + 128]
        blank = jnp.zeros_like(query)
        outs = []
        for head in (0, 1):
            own = jnp.where(first, query, blank) if head == 0 else jnp.where(first, blank, query)
            probs = probs_of(own, keys, slopes[2 * two + head], apart, same)
            outs.append(dot(probs.astype(LOW), values))
        attended[:, lanes] = jnp.where(first, outs[0], outs[1]).astype(LOW)
    half = width // 2
    halves(section, attended[...], pack_near.at[:, :half], pack_far.at[:, :half])
    total = merged[...] + dot(pack_near[:, :half], read_near[...])
    total = total + dot(pack_far[:, :half], read_far[...])
    residual[...] = total
    xhat, _ = nrm_stats(total)
    gain = vector(section, near_v, far_v, width, width // 2)
    bias = vector(section, near_v, far_v, width + width // 2, width // 2)
    second = (xhat * gain + bias).astype(LOW)
    halves(section, second, pack_near.at[:, half:], pack_far.at[:, half:])


def feed_kernel(
    where, pack_near, pack_far, top, residual, near_v, far_v, up_near, up_far, down_near, down_far,
    act_near, act_far, lifted_t, up_bias_grad, output, residual_grad, residual_low, residual_t,
    gain_grad, bias_grad, out_sum, grad_sum,
):
    section = where[0]
    step, steps = pl.program_id(0), pl.num_programs(0)

    @pl.when(step == 0)
    def _():
        out_sum[...] = jnp.zeros_like(out_sum)
        grad_sum[...] = jnp.zeros_like(grad_sum)

    def run(down, act, packed):
        tile = up_near.shape[1]
        spot = pl.multiple_of(2 * top.shape[1] + step % (steps // 2) * tile, tile)
        up_bias = packed[:, pl.ds(spot, tile)].astype(FULL)
        half = pack_near.shape[1] // 2
        lifted = dot(pack_near[:, half:], up_near[...])
        lifted = lifted + dot(pack_far[:, half:], up_far[...]) + up_bias
        square = lifted * lifted
        turn = jnp.tanh(0.7978845608028654 * lifted * (1.0 + 0.044715 * square))
        rise = 0.5 * (1.0 + turn)
        slope = rise + (0.5 * 0.7978845608028654) * lifted * (1.0 - turn * turn) * (
            1.0 + 3 * 0.044715 * square
        )
        active = (lifted * rise).astype(LOW)
        act[...] = active
        out_sum[...] += dot(active, down[...])
        lifted_grad = (contract_last(top[...], down[...]) * slope).astype(LOW)
        wide = lifted_grad.astype(FULL)
        up_bias_grad[...] = jnp.sum(wide, axis=0, keepdims=True)
        lifted_t[...] = wide.T.astype(LOW)
        part(grad_sum, section, False)[...] += contract_last(lifted_grad, up_near[...])
        part(grad_sum, section, True)[...] += contract_last(lifted_grad, up_far[...])

    @pl.when(step < steps // 2)
    def _():
        run(down_near, act_near, near_v)

    @pl.when(step >= steps // 2)
    def _():
        run(down_far, act_far, far_v)

    @pl.when(step == steps - 1)
    def _():
        before = residual[...]
        output[...] = (before + out_sum[...]).astype(LOW)
        grad = grad_sum[...]
        xhat, scale = nrm_stats(before)
        gain_grad[...] = jnp.sum(grad * xhat, axis=0, keepdims=True)
        bias_grad[...] = jnp.sum(grad, axis=0, keepdims=True)
        width = top.shape[1]
        gain = vector(section, near_v, far_v, width, width // 2)
        total = top[...].astype(FULL) + nrm_back(xhat, scale, grad, gain)
        residual_grad[...] = total
        residual_low[...] = total.astype(LOW)
        residual_t[...] = total.T.astype(LOW)


def unattend_kernel(
    where, mixed, residual_low, segments, read_near, read_far,
    mixed_grad, mixed_t, pulled,
):
    section = where[0]
    width = residual_low.shape[1]
    heads = width // HEAD_DIM
    grad = residual_low[...]
    part(pulled, section, False)[...] = contract_last(grad, read_near[...]).astype(LOW)
    part(pulled, section, True)[...] = contract_last(grad, read_far[...]).astype(LOW)
    same, apart, slopes, first = score_parts(heads, segments[...])
    for two in range(heads // 2):
        spots = [slice(k * width + two * 128, k * width + two * 128 + 128) for k in range(3)]
        query, keys, values = (mixed[:, spot] for spot in spots)
        given = pulled[:, spots[0]]
        blank = jnp.zeros_like(query)
        made = []
        for head in (0, 1):
            keep = (lambda v: jnp.where(first, v, blank)) if head == 0 else (
                lambda v: jnp.where(first, blank, v)
            )
            probs = probs_of(keep(query), keys, slopes[2 * two + head], apart, same)
            prob_grad = contract_last(keep(given), values)
            score = probs * (prob_grad - jnp.sum(probs * prob_grad, -1, keepdims=True))
            score = score.astype(LOW)
            made.append(
                (
                    dot(score, keys) * 0.125,
                    contract_first(score, query) * 0.125,
                    contract_first(probs.astype(LOW), given),
                )
            )
        for spot, one, other in zip(spots, *made):
            both = jnp.where(first, one, other)
            mixed_grad[:, spot] = both.astype(LOW)
            mixed_t[spot, :] = both.T.astype(LOW)


def unmix_kernel(
    where, mixed_grad, mix_near, mix_far, merged, residual_grad, near_v, far_v,
    merged_low, merged_t, gain_grad, bias_grad, first_grad,
):
    section = where[0]
    part(first_grad, section, False)[...] = contract_last(mixed_grad[...], mix_near[...])
    part(first_grad, section, True)[...] = contract_last(mixed_grad[...], mix_far[...])
    grad = first_grad[...]
    xhat, scale = nrm_stats(merged[...])
    gain_grad[...] = jnp.sum(grad * xhat, axis=0, keepdims=True)
    bias_grad[...] = jnp.sum(grad, axis=0, keepdims=True)
    gain = vector(section, near_v, far_v, 0, merged.shape[1] // 2)
    total = residual_grad[...] + nrm_back(xhat, scale, grad, gain)
    merged_low[...] = total.astype(LOW)
    merged_t[...] = total.T.astype(LOW)


def unmerge_kernel(where, merged_low, near_w, far_w, input_grad, skip_grad):
    near = contract_last(merged_low[...], near_w[...]).astype(LOW)
    far = contract_last(merged_low[...], far_w[...]).astype(LOW)
    input_grad[...] = jnp.where(where[0] == 0, near, far)
    skip_grad[...] = jnp.where(where[0] == 0, far, near)


def shaped(shape, kind):
    return jax.ShapeDtypeStruct(shape, kind)


def plain_call(kernel, made, operands, grant, scratch=(), scalars=0):
    cost = sum(x.size * x.dtype.itemsize for x in operands)
    specs = [pl.BlockSpec(memory_space=pltpu.SMEM)] * scalars
    specs += [pl.BlockSpec(memory_space=pltpu.VMEM)] * (len(operands) - scalars)
    return pl.pallas_call(
        kernel,
        out_shape=made,
        in_specs=specs,
        out_specs=[pl.BlockSpec(memory_space=pltpu.VMEM)] * len(made),
        scratch_shapes=list(scratch),
        compiler_params=pltpu.CompilerParams(vmem_limit_bytes=grant << 20),
        cost_estimate=pl.CostEstimate(
            flops=128 * cost, bytes_accessed=cost, transcendentals=0
        ),
    )(*operands)


def feed_call(where, pack_near, pack_far, top, residual, near_v, far_v, up_near, up_far, down_near, down_far):
    rows, width = top.shape
    hidden = up_near.shape[1]
    steps = 4
    tile, last = hidden // steps, steps // 2 - 1
    half = width // 2

    def whole(*shape):
        return pl.BlockSpec(shape, lambda j, w: (0,) * len(shape))

    def spot(j, w):
        return (j // (steps // 2) + w[0]) % 2 * (steps // 2) + j % (steps // 2)

    def near(j):
        return jnp.minimum(j, last)

    def far(j):
        return jnp.maximum(j - last - 1, 0)

    in_specs = [
        whole(rows, width), whole(rows, width), whole(rows, width), whole(rows, width),
        whole(*near_v.shape), whole(*far_v.shape),
        pl.BlockSpec((half, tile), lambda j, w: (0, spot(j, w))),
        pl.BlockSpec((half, tile), lambda j, w: (0, spot(j, w))),
        pl.BlockSpec((tile, width), lambda j, w: (near(j), 0)),
        pl.BlockSpec((tile, width), lambda j, w: (far(j), 0)),
    ]
    out_specs = [
        pl.BlockSpec((rows, tile), lambda j, w: (0, near(j))),
        pl.BlockSpec((rows, tile), lambda j, w: (0, far(j))),
        pl.BlockSpec((tile, rows), lambda j, w: (spot(j, w), 0)),
        pl.BlockSpec((1, tile), lambda j, w: (0, spot(j, w))),
        whole(rows, width), whole(rows, width), whole(rows, width), whole(width, rows),
        whole(1, width), whole(1, width),
    ]
    made = [
        shaped((rows, hidden // 2), LOW), shaped((rows, hidden // 2), LOW),
        shaped((hidden, rows), LOW), shaped((1, hidden), FULL),
        shaped((rows, width), LOW), shaped((rows, width), FULL), shaped((rows, width), LOW),
        shaped((width, rows), LOW), shaped((1, width), FULL), shaped((1, width), FULL),
    ]
    weights = 4 * width * hidden
    return pl.pallas_call(
        feed_kernel,
        out_shape=made,
        grid_spec=pltpu.PrefetchScalarGridSpec(
            num_scalar_prefetch=1,
            grid=(steps,),
            in_specs=in_specs,
            out_specs=out_specs,
            scratch_shapes=[pltpu.VMEM((rows, width), FULL)] * 2,
        ),
        compiler_params=pltpu.CompilerParams(
            dimension_semantics=("arbitrary",), vmem_limit_bytes=24 << 20
        ),
        cost_estimate=pl.CostEstimate(
            flops=4 * rows * weights, bytes_accessed=weights, transcendentals=rows * hidden
        ),
        name="feed",
    )(where, pack_near, pack_far, top, residual, near_v, far_v, up_near, up_far, down_near, down_far)


def pick(value, spot, axis=0):
    return lax.dynamic_index_in_dim(value, spot, axis, keepdims=False)


def gather_left(torus, axes, own, far):
    chip = jnp.concatenate([own, far], axis=0)
    lead = torus.order(axes)[0]
    return jnp.concatenate([chip, torus.flip(chip, lead)], axis=0)


def gather_right(torus, axis, own):
    lead, rest = torus.order(axis)
    columns, tokens = own.shape
    split = own.reshape(*(2,) * torus.power, columns // torus.count, tokens)
    place = [torus.power - 1 - bit for bit in (lead, *rest)]
    split = split.transpose(*place, torus.power, torus.power + 1)
    split = split.reshape(2, columns // 2, tokens)
    here = torus.bit(lead)
    near = jnp.stack([pick(split, here), torus.flip(pick(split, 1 - here), lead)])
    far = pair(near)
    return jnp.concatenate([near[0], far[0], near[1], far[1]], axis=1)


def reduce_grad(torus, axis, left, right):
    rest = torus.order(axis)[1]
    halves = right.reshape(2, -1, right.shape[1])
    here = torus.bit(rest[0])
    sent = dot(pick(halves, 1 - here), left).astype(LOW)
    sent = torus.flip(sent, rest[0])
    total = dot(pick(halves, here), left) + sent.astype(FULL)
    for bit in rest[1:]:
        here = torus.bit(bit)
        held = total.astype(LOW).reshape(2, -1, left.shape[1])
        sent = torus.flip(pick(held, 1 - here), bit)
        total = pick(held, here).astype(FULL) + sent.astype(FULL)
    return total


def body(
    layer_input,
    skip_input,
    segment_ids,
    out_cotangent,
    merger,
    mixing,
    readout,
    expand,
    narrow,
    first_gain,
    first_bias,
    second_gain,
    second_bias,
    up_bias,
):
    torus = Torus(lax.axis_size("dp"))
    section = lax.axis_index("section")
    rows, width = layer_input.shape
    first_core = section == 0

    def packed(parts):
        bounds, total = [], 0
        for item in parts:
            bounds.append((total, total + item.shape[0]))
            total += item.shape[0]
        placed = [jnp.pad(item, (low, total - high)) for item, (low, high) in zip(parts, bounds)]
        return sum(placed[1:], placed[0]), bounds

    def mine(value):
        half = value.shape[-1] // 2
        return lax.dynamic_slice_in_dim(value, section * half, half, value.ndim - 1)

    merger_far = pair(merger)
    near_v, _ = packed((first_gain, first_bias, second_gain, second_bias, up_bias))
    near_v = near_v[None]
    far_v = pair(near_v)
    mixing_far = pair(mixing)
    readout_far = pair(readout)
    expand_far = pair(expand)
    narrow_far = pair(narrow)
    top_low = pair(out_cotangent)

    where = section.astype(jnp.int32).reshape(1)
    frames_mine = jnp.where(first_core, layer_input, skip_input)
    frames_other = jnp.where(first_core, skip_input, layer_input)
    segments = pick(segment_ids[0], section)[None]
    flat, tall, thin = (rows, width), (width, rows), (rows, width // 2)
    line = shaped((1, width), FULL)

    merged, low_near, low_far, top_t = plain_call(
        merge_kernel,
        [shaped(flat, FULL), shaped(thin, LOW), shaped(thin, LOW), shaped(tall, LOW)],
        (where, layer_input, skip_input, merger, merger_far, near_v, far_v, top_low), 12, scalars=1,
    )
    mixed, pack_near, pack_far, residual = plain_call(
        attend_kernel,
        [shaped((rows, 3 * width), LOW), shaped(flat, LOW), shaped(flat, LOW), shaped(flat, FULL)],
        (where, low_near, low_far, merged, segments, mixing, mixing_far, readout, readout_far,
         near_v, far_v),
        24, scratch=[pltpu.VMEM(flat, LOW)], scalars=1,
    )
    (act_near, act_far, lifted_t, up_bias_grad, output, residual_grad, residual_low, residual_t,
     second_gain_grad, second_bias_grad) = feed_call(
        where, pack_near, pack_far, top_low, residual, near_v, far_v, expand, expand_far, narrow,
        narrow_far,
    )
    block_output = pair(output)
    mixed_grad, mixed_t = plain_call(
        unattend_kernel,
        [shaped((rows, 3 * width), LOW), shaped((3 * width, rows), LOW)],
        (where, mixed, residual_low, segments, readout, readout_far),
        16, scratch=[pltpu.VMEM(flat, LOW)], scalars=1,
    )
    merged_low, merged_t, first_gain_grad, first_bias_grad = plain_call(
        unmix_kernel, [shaped(flat, LOW), shaped(tall, LOW), line, line],
        (where, mixed_grad, mixing, mixing_far, merged, residual_grad, near_v, far_v),
        16, scratch=[pltpu.VMEM(flat, FULL)], scalars=1,
    )
    input_grad, skip_grad = plain_call(
        unmerge_kernel, [shaped(flat, LOW)] * 2,
        (where, merged_low, merger, merger_far), 12, scalars=1,
    )

    def left_of(axes, near, far):
        return gather_left(torus, axes, near, pair(far))

    def grad_of(axes, left, right_t):
        return reduce_grad(torus, axes, left, gather_right(torus, axes, right_t))

    half = width // 2
    merger_left = left_of("yzx", frames_mine, frames_other)
    mixing_left = left_of("Zxy", low_near, low_far)
    mid_left = left_of("zxy", pack_near, pack_far)
    narrow_left = left_of("xyz", act_near, act_far)
    narrow_grad = grad_of("xyz", narrow_left, top_t)
    expand_grad = grad_of("zxy", mid_left[:, half:], lifted_t)
    readout_grad = grad_of("zyx", mid_left[:, :half], residual_t)
    mixing_grad = grad_of("Zxy", mixing_left, mixed_t)
    merger_grad = grad_of("yzx", merger_left, merged_t)

    small, bounds = packed(
        [
            item[0]
            for item in (
                first_gain_grad, first_bias_grad, second_gain_grad, second_bias_grad, up_bias_grad
            )
        ]
    )
    small = small.reshape(-1, 128)
    small = small + pair(small)
    for bit in torus.bits["z"] + torus.bits["x"] + torus.bits["y"]:
        small = small + torus.flip(small, bit)
    small = small.reshape(-1)
    merger_out = merger_grad.T
    matrices = (merger_out, mixing_grad.T, readout_grad.T, expand_grad.T, narrow_grad.T)
    return (block_output, input_grad, skip_grad) + matrices + tuple(
        mine(small[low:high]) for low, high in bounds
    )


def solution(mesh):
    tokens = P(("section", "dp"), None)
    matrix, vector = P("section", None), P("section")
    placed = (tokens, tokens, P("dp", None, None), tokens) + (matrix,) * 5 + (vector,) * 5
    made = (tokens,) * 3 + (P("section", "dp"),) * 5 + (vector,) * 5
    return jax.shard_map(body, mesh=mesh, in_specs=placed, out_specs=made, check_vma=False)
```

```python
import jax
import jax.numpy as jnp
from jax import lax
from jax.experimental import pallas as pl
from jax.experimental.pallas import tpu as pltpu
from jax.sharding import PartitionSpec as P


HEAD_DIM = 64
LOW = jnp.bfloat16
FULL = jnp.float32


class Torus:
    def __init__(self, count):
        power = count.bit_length() - 1
        side = power // 3
        self.count, self.power = count, power
        self.bits = {
            "x": list(range(side)),
            "y": list(range(side, 2 * side)),
            "z": list(range(2 * side, power)),
        }

    def order(self, axes):
        lead = self.bits[axes[0].lower()]
        if axes[0].isupper():
            lead = lead[::-1]
        return lead[0], self.bits[axes[1]] + self.bits[axes[2]] + lead[1:]

    def bit(self, bit):
        return (lax.axis_index("dp") >> bit) & 1

    def flip(self, value, bit):
        pairs = [(source, source ^ (1 << bit)) for source in range(self.count)]
        return lax.ppermute(value, "dp", pairs)


def pair(value):
    return lax.ppermute(value, "section", [(0, 1), (1, 0)])


def dot(left, right):
    return jnp.dot(left, right, preferred_element_type=FULL)


def contract_first(left, right):
    return lax.dot_general(left, right, (((0,), (0,)), ((), ())), preferred_element_type=FULL)


def contract_last(left, right):
    return lax.dot_general(left, right, (((1,), (1,)), ((), ())), preferred_element_type=FULL)


def nrm_stats(values):
    center = values - jnp.mean(values, -1, keepdims=True)
    scale = lax.rsqrt(jnp.mean(center * center, -1, keepdims=True) + 1e-05)
    return center * scale, scale


def nrm_back(xhat, scale, grad, gain):
    g = grad * gain
    inner = g - jnp.mean(g, -1, keepdims=True) - xhat * jnp.mean(g * xhat, -1, keepdims=True)
    return scale * inner


def part(ref, section, far):
    half = ref.shape[1] // 2
    spot = (1 - section) if far else section
    return ref.at[:, pl.ds(pl.multiple_of(spot * half, half), half)]


def vector(section, near, far, low, size):
    one, two = near[:, low : low + size].astype(FULL), far[:, low : low + size].astype(FULL)
    return jnp.where(
        section == 0, jnp.concatenate([one, two], axis=1), jnp.concatenate([two, one], axis=1)
    )


def halves(section, values, near, far):
    half = values.shape[1] // 2
    one, two = values[:, :half], values[:, half:]
    near[...] = jnp.where(section == 0, one, two)
    far[...] = jnp.where(section == 0, two, one)


def merge_kernel(
    where, first_x, second_x, near_w, far_w, near_v, far_v, top,
    merged, low_near, low_far, top_t,
):
    half = first_x.shape[1] // 2
    near_x = jnp.where(where[0] == 0, first_x[...], second_x[...])
    far_x = jnp.where(where[0] == 0, second_x[...], first_x[...])
    gain = vector(where[0], near_v, far_v, 0, half)
    bias = vector(where[0], near_v, far_v, half, half)
    total = dot(near_x, near_w[...]) + dot(far_x, far_w[...])
    merged[...] = total
    xhat, _ = nrm_stats(total)
    halves(where[0], (xhat * gain + bias).astype(LOW), low_near, low_far)
    top_t[...] = top[...].astype(FULL).T.astype(LOW)


def score_parts(heads, segments):
    rows = segments.shape[1]
    spread = jnp.broadcast_to(segments.astype(FULL), (rows, rows))
    same = spread == spread.T
    spots = [lax.broadcasted_iota(jnp.int32, (rows, rows), axis) for axis in (0, 1)]
    apart = jnp.abs(spots[0] - spots[1]).astype(FULL)
    slopes = [2.0 ** (-8.0 * (head + 1) / heads) for head in range(heads)]
    lane = lax.broadcasted_iota(jnp.int32, (rows, 2 * HEAD_DIM), 1)
    return same, apart, slopes, lane < HEAD_DIM


def probs_of(query, keys, slope, apart, same):
    raw = contract_last(query, keys) * 0.125 - slope * apart
    raw = jnp.where(same, raw, -1000000000.0)
    raised = jnp.exp(raw - jnp.max(raw, -1, keepdims=True))
    return raised / jnp.sum(raised, -1, keepdims=True)


def attend_kernel(
    where, near_low, far_low, merged, segments, mix_near, mix_far, read_near, read_far, near_v, far_v,
    mixed, pack_near, pack_far, residual, attended,
):
    section = where[0]
    width = merged.shape[1]
    heads = width // HEAD_DIM
    near, far = near_low[...], far_low[...]
    step = width // 2
    for base in range(0, 3 * width, step):
        block = dot(near, mix_near[:, base : base + step]) + dot(far, mix_far[:, base : base + step])
        mixed[:, base : base + step] = block.astype(LOW)
    same, apart, slopes, first = score_parts(heads, segments[...])
    for two in range(heads // 2):
        lanes = slice(two * 128, two * 128 + 128)
        query = mixed[:, lanes]
        keys = mixed[:, width + two * 128 : width + two * 128 + 128]
        values = mixed[:, 2 * width + two * 128 : 2 * width + two * 128 + 128]
        blank = jnp.zeros_like(query)
        outs = []
        for head in (0, 1):
            own = jnp.where(first, query, blank) if head == 0 else jnp.where(first, blank, query)
            probs = probs_of(own, keys, slopes[2 * two + head], apart, same)
            outs.append(dot(probs.astype(LOW), values))
        attended[:, lanes] = jnp.where(first, outs[0], outs[1]).astype(LOW)
    half = width // 2
    halves(section, attended[...], pack_near.at[:, :half], pack_far.at[:, :half])
    total = merged[...] + dot(pack_near[:, :half], read_near[...])
    total = total + dot(pack_far[:, :half], read_far[...])
    residual[...] = total
    xhat, _ = nrm_stats(total)
    gain = vector(section, near_v, far_v, width, width // 2)
    bias = vector(section, near_v, far_v, width + width // 2, width // 2)
    second = (xhat * gain + bias).astype(LOW)
    halves(section, second, pack_near.at[:, half:], pack_far.at[:, half:])


def feed_kernel(
    where, pack_near, pack_far, top, residual, near_v, far_v, up_near, up_far, down_near, down_far,
    act_near, act_far, lifted_t, up_bias_grad, output, residual_grad, residual_low, residual_t,
    gain_grad, bias_grad, out_sum, grad_sum,
):
    section = where[0]
    step, steps = pl.program_id(0), pl.num_programs(0)

    @pl.when(step == 0)
    def _():
        out_sum[...] = jnp.zeros_like(out_sum)
        grad_sum[...] = jnp.zeros_like(grad_sum)

    def run(down, act, packed):
        tile = up_near.shape[1]
        spot = pl.multiple_of(2 * top.shape[1] + step % (steps // 2) * tile, tile)
        up_bias = packed[:, pl.ds(spot, tile)].astype(FULL)
        half = pack_near.shape[1] // 2
        lifted = dot(pack_near[:, half:], up_near[...])
        lifted = lifted + dot(pack_far[:, half:], up_far[...]) + up_bias
        square = lifted * lifted
        turn = jnp.tanh(0.7978845608028654 * lifted * (1.0 + 0.044715 * square))
        rise = 0.5 * (1.0 + turn)
        slope = rise + (0.5 * 0.7978845608028654) * lifted * (1.0 - turn * turn) * (
            1.0 + 3 * 0.044715 * square
        )
        active = (lifted * rise).astype(LOW)
        act[...] = active
        out_sum[...] += dot(active, down[...])
        lifted_grad = (contract_last(top[...], down[...]) * slope).astype(LOW)
        wide = lifted_grad.astype(FULL)
        up_bias_grad[...] = jnp.sum(wide, axis=0, keepdims=True)
        lifted_t[...] = wide.T.astype(LOW)
        part(grad_sum, section, False)[...] += contract_last(lifted_grad, up_near[...])
        part(grad_sum, section, True)[...] += contract_last(lifted_grad, up_far[...])

    @pl.when(step < steps // 2)
    def _():
        run(down_near, act_near, near_v)

    @pl.when(step >= steps // 2)
    def _():
        run(down_far, act_far, far_v)

    @pl.when(step == steps - 1)
    def _():
        before = residual[...]
        output[...] = (before + out_sum[...]).astype(LOW)
        grad = grad_sum[...]
        xhat, scale = nrm_stats(before)
        gain_grad[...] = jnp.sum(grad * xhat, axis=0, keepdims=True)
        bias_grad[...] = jnp.sum(grad, axis=0, keepdims=True)
        width = top.shape[1]
        gain = vector(section, near_v, far_v, width, width // 2)
        total = top[...].astype(FULL) + nrm_back(xhat, scale, grad, gain)
        residual_grad[...] = total
        residual_low[...] = total.astype(LOW)
        residual_t[...] = total.T.astype(LOW)


def unattend_kernel(
    where, mixed, residual_low, segments, read_near, read_far,
    mixed_grad, mixed_t, pulled,
):
    section = where[0]
    width = residual_low.shape[1]
    heads = width // HEAD_DIM
    grad = residual_low[...]
    part(pulled, section, False)[...] = contract_last(grad, read_near[...]).astype(LOW)
    part(pulled, section, True)[...] = contract_last(grad, read_far[...]).astype(LOW)
    same, apart, slopes, first = score_parts(heads, segments[...])
    for two in range(heads // 2):
        spots = [slice(k * width + two * 128, k * width + two * 128 + 128) for k in range(3)]
        query, keys, values = (mixed[:, spot] for spot in spots)
        given = pulled[:, spots[0]]
        blank = jnp.zeros_like(query)
        made = []
        for head in (0, 1):
            keep = (lambda v: jnp.where(first, v, blank)) if head == 0 else (
                lambda v: jnp.where(first, blank, v)
            )
            probs = probs_of(keep(query), keys, slopes[2 * two + head], apart, same)
            prob_grad = contract_last(keep(given), values)
            score = probs * (prob_grad - jnp.sum(probs * prob_grad, -1, keepdims=True))
            score = score.astype(LOW)
            made.append(
                (
                    dot(score, keys) * 0.125,
                    contract_first(score, query) * 0.125,
                    contract_first(probs.astype(LOW), given),
                )
            )
        for spot, one, other in zip(spots, *made):
            both = jnp.where(first, one, other)
            mixed_grad[:, spot] = both.astype(LOW)
            mixed_t[spot, :] = both.T.astype(LOW)


def unmix_kernel(
    where, mixed_grad, mix_near, mix_far, merged, residual_grad, near_v, far_v,
    merged_low, merged_t, gain_grad, bias_grad, first_grad,
):
    section = where[0]
    part(first_grad, section, False)[...] = contract_last(mixed_grad[...], mix_near[...])
    part(first_grad, section, True)[...] = contract_last(mixed_grad[...], mix_far[...])
    grad = first_grad[...]
    xhat, scale = nrm_stats(merged[...])
    gain_grad[...] = jnp.sum(grad * xhat, axis=0, keepdims=True)
    bias_grad[...] = jnp.sum(grad, axis=0, keepdims=True)
    gain = vector(section, near_v, far_v, 0, merged.shape[1] // 2)
    total = residual_grad[...] + nrm_back(xhat, scale, grad, gain)
    merged_low[...] = total.astype(LOW)
    merged_t[...] = total.T.astype(LOW)


def unmerge_kernel(where, merged_low, near_w, far_w, input_grad, skip_grad):
    near = contract_last(merged_low[...], near_w[...]).astype(LOW)
    far = contract_last(merged_low[...], far_w[...]).astype(LOW)
    input_grad[...] = jnp.where(where[0] == 0, near, far)
    skip_grad[...] = jnp.where(where[0] == 0, far, near)


def shaped(shape, kind):
    return jax.ShapeDtypeStruct(shape, kind)


def plain_call(kernel, made, operands, grant, scratch=(), scalars=0):
    cost = sum(x.size * x.dtype.itemsize for x in operands)
    specs = [pl.BlockSpec(memory_space=pltpu.SMEM)] * scalars
    specs += [pl.BlockSpec(memory_space=pltpu.VMEM)] * (len(operands) - scalars)
    return pl.pallas_call(
        kernel,
        out_shape=made,
        in_specs=specs,
        out_specs=[pl.BlockSpec(memory_space=pltpu.VMEM)] * len(made),
        scratch_shapes=list(scratch),
        compiler_params=pltpu.CompilerParams(vmem_limit_bytes=grant << 20),
        cost_estimate=pl.CostEstimate(
            flops=128 * cost, bytes_accessed=cost, transcendentals=0
        ),
    )(*operands)


def feed_call(where, pack_near, pack_far, top, residual, near_v, far_v, up_near, up_far, down_near, down_far):
    rows, width = top.shape
    hidden = up_near.shape[1]
    steps = 4
    tile, last = hidden // steps, steps // 2 - 1
    half = width // 2

    def whole(*shape):
        return pl.BlockSpec(shape, lambda j, w: (0,) * len(shape))

    def spot(j, w):
        return (j // (steps // 2) + w[0]) % 2 * (steps // 2) + j % (steps // 2)

    def near(j):
        return jnp.minimum(j, last)

    def far(j):
        return jnp.maximum(j - last - 1, 0)

    in_specs = [
        whole(rows, width), whole(rows, width), whole(rows, width), whole(rows, width),
        whole(*near_v.shape), whole(*far_v.shape),
        pl.BlockSpec((half, tile), lambda j, w: (0, spot(j, w))),
        pl.BlockSpec((half, tile), lambda j, w: (0, spot(j, w))),
        pl.BlockSpec((tile, width), lambda j, w: (near(j), 0)),
        pl.BlockSpec((tile, width), lambda j, w: (far(j), 0)),
    ]
    out_specs = [
        pl.BlockSpec((rows, tile), lambda j, w: (0, near(j))),
        pl.BlockSpec((rows, tile), lambda j, w: (0, far(j))),
        pl.BlockSpec((tile, rows), lambda j, w: (spot(j, w), 0)),
        pl.BlockSpec((1, tile), lambda j, w: (0, spot(j, w))),
        whole(rows, width), whole(rows, width), whole(rows, width), whole(width, rows),
        whole(1, width), whole(1, width),
    ]
    made = [
        shaped((rows, hidden // 2), LOW), shaped((rows, hidden // 2), LOW),
        shaped((hidden, rows), LOW), shaped((1, hidden), FULL),
        shaped((rows, width), LOW), shaped((rows, width), FULL), shaped((rows, width), LOW),
        shaped((width, rows), LOW), shaped((1, width), FULL), shaped((1, width), FULL),
    ]
    weights = 4 * width * hidden
    return pl.pallas_call(
        feed_kernel,
        out_shape=made,
        grid_spec=pltpu.PrefetchScalarGridSpec(
            num_scalar_prefetch=1,
            grid=(steps,),
            in_specs=in_specs,
            out_specs=out_specs,
            scratch_shapes=[pltpu.VMEM((rows, width), FULL)] * 2,
        ),
        compiler_params=pltpu.CompilerParams(
            dimension_semantics=("arbitrary",), vmem_limit_bytes=24 << 20
        ),
        cost_estimate=pl.CostEstimate(
            flops=4 * rows * weights, bytes_accessed=weights, transcendentals=rows * hidden
        ),
        name="feed",
    )(where, pack_near, pack_far, top, residual, near_v, far_v, up_near, up_far, down_near, down_far)


def pick(value, spot, axis=0):
    return lax.dynamic_index_in_dim(value, spot, axis, keepdims=False)


def gather_left(torus, axes, own, far):
    chip = jnp.concatenate([own, far], axis=0)
    lead = torus.order(axes)[0]
    return jnp.concatenate([chip, torus.flip(chip, lead)], axis=0)


def gather_right(torus, axis, own):
    lead, rest = torus.order(axis)
    columns, tokens = own.shape
    split = own.reshape(*(2,) * torus.power, columns // torus.count, tokens)
    place = [torus.power - 1 - bit for bit in (lead, *rest)]
    split = split.transpose(*place, torus.power, torus.power + 1)
    split = split.reshape(2, columns // 2, tokens)
    here = torus.bit(lead)
    near = jnp.stack([pick(split, here), torus.flip(pick(split, 1 - here), lead)])
    far = pair(near)
    return jnp.concatenate([near[0], far[0], near[1], far[1]], axis=1)


def reduce_grad(torus, axis, left, right):
    rest = torus.order(axis)[1]
    halves = right.reshape(2, -1, right.shape[1])
    here = torus.bit(rest[0])
    sent = dot(pick(halves, 1 - here), left).astype(LOW)
    sent = torus.flip(sent, rest[0])
    total = dot(pick(halves, here), left) + sent.astype(FULL)
    for bit in rest[1:]:
        here = torus.bit(bit)
        held = total.astype(LOW).reshape(2, -1, left.shape[1])
        sent = torus.flip(pick(held, 1 - here), bit)
        total = pick(held, here).astype(FULL) + sent.astype(FULL)
    return total


def body(
    layer_input,
    skip_input,
    segment_ids,
    out_cotangent,
    merger,
    mixing,
    readout,
    expand,
    narrow,
    first_gain,
    first_bias,
    second_gain,
    second_bias,
    up_bias,
):
    torus = Torus(lax.axis_size("dp"))
    section = lax.axis_index("section")
    rows, width = layer_input.shape
    first_core = section == 0

    def packed(parts):
        bounds, total = [], 0
        for item in parts:
            bounds.append((total, total + item.shape[0]))
            total += item.shape[0]
        placed = [jnp.pad(item, (low, total - high)) for item, (low, high) in zip(parts, bounds)]
        return sum(placed[1:], placed[0]), bounds

    def mine(value):
        half = value.shape[-1] // 2
        return lax.dynamic_slice_in_dim(value, section * half, half, value.ndim - 1)

    merger_far = pair(merger)
    near_v, _ = packed((first_gain, first_bias, second_gain, second_bias, up_bias))
    near_v = near_v[None]
    far_v = pair(near_v)
    mixing_far = pair(mixing)
    readout_far = pair(readout)
    expand_far = pair(expand)
    narrow_far = pair(narrow)
    top_low = pair(out_cotangent)

    where = section.astype(jnp.int32).reshape(1)
    frames_mine = jnp.where(first_core, layer_input, skip_input)
    frames_other = jnp.where(first_core, skip_input, layer_input)
    segments = pick(segment_ids[0], section)[None]
    flat, tall, thin = (rows, width), (width, rows), (rows, width // 2)
    line = shaped((1, width), FULL)

    merged, low_near, low_far, top_t = plain_call(
        merge_kernel,
        [shaped(flat, FULL), shaped(thin, LOW), shaped(thin, LOW), shaped(tall, LOW)],
        (where, layer_input, skip_input, merger, merger_far, near_v, far_v, top_low), 56, scalars=1,
    )
    mixed, pack_near, pack_far, residual = plain_call(
        attend_kernel,
        [shaped((rows, 3 * width), LOW), shaped(flat, LOW), shaped(flat, LOW), shaped(flat, FULL)],
        (where, low_near, low_far, merged, segments, mixing, mixing_far, readout, readout_far,
         near_v, far_v),
        24, scratch=[pltpu.VMEM(flat, LOW)], scalars=1,
    )
    (act_near, act_far, lifted_t, up_bias_grad, output, residual_grad, residual_low, residual_t,
     second_gain_grad, second_bias_grad) = feed_call(
        where, pack_near, pack_far, top_low, residual, near_v, far_v, expand, expand_far, narrow,
        narrow_far,
    )
    block_output = pair(output)
    mixed_grad, mixed_t = plain_call(
        unattend_kernel,
        [shaped((rows, 3 * width), LOW), shaped((3 * width, rows), LOW)],
        (where, mixed, residual_low, segments, readout, readout_far),
        16, scratch=[pltpu.VMEM(flat, LOW)], scalars=1,
    )
    merged_low, merged_t, first_gain_grad, first_bias_grad = plain_call(
        unmix_kernel, [shaped(flat, LOW), shaped(tall, LOW), line, line],
        (where, mixed_grad, mixing, mixing_far, merged, residual_grad, near_v, far_v),
        16, scratch=[pltpu.VMEM(flat, FULL)], scalars=1,
    )
    input_grad, skip_grad = plain_call(
        unmerge_kernel, [shaped(flat, LOW)] * 2,
        (where, merged_low, merger, merger_far), 12, scalars=1,
    )

    def left_of(axes, near, far):
        return gather_left(torus, axes, near, pair(far))

    def grad_of(axes, left, right_t):
        return reduce_grad(torus, axes, left, gather_right(torus, axes, right_t))

    half = width // 2
    merger_left = left_of("yxz", frames_mine, frames_other)
    mixing_left = left_of("Zxy", low_near, low_far)
    mid_left = left_of("zxy", pack_near, pack_far)
    narrow_left = left_of("xyz", act_near, act_far)
    narrow_grad = grad_of("xyz", narrow_left, top_t)
    expand_grad = grad_of("zxy", mid_left[:, half:], lifted_t)
    readout_grad = grad_of("zyx", mid_left[:, :half], residual_t)
    mixing_grad = grad_of("Zxy", mixing_left, mixed_t)
    merger_grad = grad_of("yxz", merger_left, merged_t)

    small, bounds = packed(
        [
            item[0]
            for item in (
                first_gain_grad, first_bias_grad, second_gain_grad, second_bias_grad, up_bias_grad
            )
        ]
    )
    small = small.reshape(-1, 128)
    small = small + pair(small)
    for bit in torus.bits["z"] + torus.bits["x"] + torus.bits["y"]:
        small = small + torus.flip(small, bit)
    small = small.reshape(-1)
    expand_out = expand_grad.T
    matrices = (merger_grad.T, mixing_grad.T, readout_grad.T, expand_out, narrow_grad.T)
    return (block_output, input_grad, skip_grad) + matrices + tuple(
        mine(small[low:high]) for low, high in bounds
    )


def solution(mesh):
    tokens = P(("section", "dp"), None)
    matrix, vector = P("section", None), P("section")
    placed = (tokens, tokens, P("dp", None, None), tokens) + (matrix,) * 5 + (vector,) * 5
    made = (tokens,) * 3 + (P("section", "dp"),) * 5 + (vector,) * 5
    return jax.shard_map(body, mesh=mesh, in_specs=placed, out_specs=made, check_vma=False)
```

```python
import jax
import jax.numpy as jnp
from jax import lax
from jax.experimental import pallas as pl
from jax.experimental.pallas import tpu as pltpu
from jax.sharding import PartitionSpec as P


HEAD_DIM = 64
LOW = jnp.bfloat16
FULL = jnp.float32


class Torus:
    def __init__(self, count):
        power = count.bit_length() - 1
        side = power // 3
        self.count, self.power = count, power
        self.bits = {
            "x": list(range(side)),
            "y": list(range(side, 2 * side)),
            "z": list(range(2 * side, power)),
        }

    def order(self, axes):
        lead = self.bits[axes[0].lower()]
        if axes[0].isupper():
            lead = lead[::-1]
        rest = [self.bits[axis] if axis != axes[0].lower() else lead[1:] for axis in axes[1:]]
        return lead[0], sum(rest, [])

    def bit(self, bit):
        return (lax.axis_index("dp") >> bit) & 1

    def flip(self, value, bit):
        pairs = [(source, source ^ (1 << bit)) for source in range(self.count)]
        return lax.ppermute(value, "dp", pairs)


def pair(value):
    return lax.ppermute(value, "section", [(0, 1), (1, 0)])


def dot(left, right):
    return jnp.dot(left, right, preferred_element_type=FULL)


def contract_first(left, right):
    return lax.dot_general(left, right, (((0,), (0,)), ((), ())), preferred_element_type=FULL)


def contract_last(left, right):
    return lax.dot_general(left, right, (((1,), (1,)), ((), ())), preferred_element_type=FULL)


def nrm_stats(values):
    center = values - jnp.mean(values, -1, keepdims=True)
    scale = lax.rsqrt(jnp.mean(center * center, -1, keepdims=True) + 1e-05)
    return center * scale, scale


def nrm_back(xhat, scale, grad, gain):
    g = grad * gain
    inner = g - jnp.mean(g, -1, keepdims=True) - xhat * jnp.mean(g * xhat, -1, keepdims=True)
    return scale * inner


def part(ref, section, far):
    half = ref.shape[1] // 2
    spot = (1 - section) if far else section
    return ref.at[:, pl.ds(pl.multiple_of(spot * half, half), half)]


def vector(section, near, far, low, size):
    one, two = near[:, low : low + size].astype(FULL), far[:, low : low + size].astype(FULL)
    return jnp.where(
        section == 0, jnp.concatenate([one, two], axis=1), jnp.concatenate([two, one], axis=1)
    )


def halves(section, values, near, far):
    half = values.shape[1] // 2
    one, two = values[:, :half], values[:, half:]
    near[...] = jnp.where(section == 0, one, two)
    far[...] = jnp.where(section == 0, two, one)


def merge_kernel(
    where, first_x, second_x, near_w, far_w, near_v, far_v, top,
    merged, low_near, low_far, top_t,
):
    half = first_x.shape[1] // 2
    near_x = jnp.where(where[0] == 0, first_x[...], second_x[...])
    far_x = jnp.where(where[0] == 0, second_x[...], first_x[...])
    gain = vector(where[0], near_v, far_v, 0, half)
    bias = vector(where[0], near_v, far_v, half, half)
    total = dot(near_x, near_w[...]) + dot(far_x, far_w[...])
    merged[...] = total
    xhat, _ = nrm_stats(total)
    halves(where[0], (xhat * gain + bias).astype(LOW), low_near, low_far)
    top_t[...] = top[...].astype(FULL).T.astype(LOW)


def score_parts(heads, segments):
    rows = segments.shape[1]
    spread = jnp.broadcast_to(segments.astype(FULL), (rows, rows))
    same = spread == spread.T
    spots = [lax.broadcasted_iota(jnp.int32, (rows, rows), axis) for axis in (0, 1)]
    apart = jnp.abs(spots[0] - spots[1]).astype(FULL)
    slopes = [2.0 ** (-8.0 * (head + 1) / heads) for head in range(heads)]
    lane = lax.broadcasted_iota(jnp.int32, (rows, 2 * HEAD_DIM), 1)
    return same, apart, slopes, lane < HEAD_DIM


def probs_of(query, keys, slope, apart, same):
    raw = contract_last(query, keys) * 0.125 - slope * apart
    raw = jnp.where(same, raw, -1000000000.0)
    raised = jnp.exp(raw - jnp.max(raw, -1, keepdims=True))
    return raised / jnp.sum(raised, -1, keepdims=True)


def attend_kernel(
    where, near_low, far_low, merged, segments, mix_near, mix_far, read_near, read_far, near_v, far_v,
    mixed, pack_near, pack_far, residual, attended,
):
    section = where[0]
    width = merged.shape[1]
    heads = width // HEAD_DIM
    near, far = near_low[...], far_low[...]
    step = width // 2
    for base in range(0, 3 * width, step):
        block = dot(near, mix_near[:, base : base + step]) + dot(far, mix_far[:, base : base + step])
        mixed[:, base : base + step] = block.astype(LOW)
    same, apart, slopes, first = score_parts(heads, segments[...])
    for two in range(heads // 2):
        lanes = slice(two * 128, two * 128 + 128)
        query = mixed[:, lanes]
        keys = mixed[:, width + two * 128 : width + two * 128 + 128]
        values = mixed[:, 2 * width + two * 128 : 2 * width + two * 128 + 128]
        blank = jnp.zeros_like(query)
        outs = []
        for head in (0, 1):
            own = jnp.where(first, query, blank) if head == 0 else jnp.where(first, blank, query)
            probs = probs_of(own, keys, slopes[2 * two + head], apart, same)
            outs.append(dot(probs.astype(LOW), values))
        attended[:, lanes] = jnp.where(first, outs[0], outs[1]).astype(LOW)
    half = width // 2
    halves(section, attended[...], pack_near.at[:, :half], pack_far.at[:, :half])
    total = merged[...] + dot(pack_near[:, :half], read_near[...])
    total = total + dot(pack_far[:, :half], read_far[...])
    residual[...] = total
    xhat, _ = nrm_stats(total)
    gain = vector(section, near_v, far_v, width, width // 2)
    bias = vector(section, near_v, far_v, width + width // 2, width // 2)
    second = (xhat * gain + bias).astype(LOW)
    halves(section, second, pack_near.at[:, half:], pack_far.at[:, half:])


def feed_kernel(
    where, pack_near, pack_far, top, residual, near_v, far_v, up_near, up_far, down_near, down_far,
    act_near, act_far, lifted_t, up_bias_grad, output, residual_grad, residual_low, residual_t,
    gain_grad, bias_grad, out_sum, grad_sum,
):
    section = where[0]
    step, steps = pl.program_id(0), pl.num_programs(0)

    @pl.when(step == 0)
    def _():
        out_sum[...] = jnp.zeros_like(out_sum)
        grad_sum[...] = jnp.zeros_like(grad_sum)

    def run(down, act, packed):
        tile = up_near.shape[1]
        spot = pl.multiple_of(2 * top.shape[1] + step % (steps // 2) * tile, tile)
        up_bias = packed[:, pl.ds(spot, tile)].astype(FULL)
        half = pack_near.shape[1] // 2
        lifted = dot(pack_near[:, half:], up_near[...])
        lifted = lifted + dot(pack_far[:, half:], up_far[...]) + up_bias
        square = lifted * lifted
        turn = jnp.tanh(0.7978845608028654 * lifted * (1.0 + 0.044715 * square))
        rise = 0.5 * (1.0 + turn)
        slope = rise + (0.5 * 0.7978845608028654) * lifted * (1.0 - turn * turn) * (
            1.0 + 3 * 0.044715 * square
        )
        active = (lifted * rise).astype(LOW)
        act[...] = active
        out_sum[...] += dot(active, down[...])
        lifted_grad = (contract_last(top[...], down[...]) * slope).astype(LOW)
        wide = lifted_grad.astype(FULL)
        up_bias_grad[...] = jnp.sum(wide, axis=0, keepdims=True)
        lifted_t[...] = wide.T.astype(LOW)
        part(grad_sum, section, False)[...] += contract_last(lifted_grad, up_near[...])
        part(grad_sum, section, True)[...] += contract_last(lifted_grad, up_far[...])

    @pl.when(step < steps // 2)
    def _():
        run(down_near, act_near, near_v)

    @pl.when(step >= steps // 2)
    def _():
        run(down_far, act_far, far_v)

    @pl.when(step == steps - 1)
    def _():
        before = residual[...]
        output[...] = (before + out_sum[...]).astype(LOW)
        grad = grad_sum[...]
        xhat, scale = nrm_stats(before)
        gain_grad[...] = jnp.sum(grad * xhat, axis=0, keepdims=True)
        bias_grad[...] = jnp.sum(grad, axis=0, keepdims=True)
        width = top.shape[1]
        gain = vector(section, near_v, far_v, width, width // 2)
        total = top[...].astype(FULL) + nrm_back(xhat, scale, grad, gain)
        residual_grad[...] = total
        residual_low[...] = total.astype(LOW)
        residual_t[...] = total.T.astype(LOW)


def unattend_kernel(
    where, mixed, residual_low, segments, read_near, read_far,
    mixed_grad, mixed_t, pulled,
):
    section = where[0]
    width = residual_low.shape[1]
    heads = width // HEAD_DIM
    grad = residual_low[...]
    part(pulled, section, False)[...] = contract_last(grad, read_near[...]).astype(LOW)
    part(pulled, section, True)[...] = contract_last(grad, read_far[...]).astype(LOW)
    same, apart, slopes, first = score_parts(heads, segments[...])
    for two in range(heads // 2):
        spots = [slice(k * width + two * 128, k * width + two * 128 + 128) for k in range(3)]
        query, keys, values = (mixed[:, spot] for spot in spots)
        given = pulled[:, spots[0]]
        blank = jnp.zeros_like(query)
        made = []
        for head in (0, 1):
            keep = (lambda v: jnp.where(first, v, blank)) if head == 0 else (
                lambda v: jnp.where(first, blank, v)
            )
            probs = probs_of(keep(query), keys, slopes[2 * two + head], apart, same)
            prob_grad = contract_last(keep(given), values)
            score = probs * (prob_grad - jnp.sum(probs * prob_grad, -1, keepdims=True))
            score = score.astype(LOW)
            made.append(
                (
                    dot(score, keys) * 0.125,
                    contract_first(score, query) * 0.125,
                    contract_first(probs.astype(LOW), given),
                )
            )
        for spot, one, other in zip(spots, *made):
            both = jnp.where(first, one, other)
            mixed_grad[:, spot] = both.astype(LOW)
            mixed_t[spot, :] = both.T.astype(LOW)


def unmix_kernel(
    where, mixed_grad, mix_near, mix_far, merged, residual_grad, near_v, far_v,
    merged_low, merged_t, gain_grad, bias_grad, first_grad,
):
    section = where[0]
    part(first_grad, section, False)[...] = contract_last(mixed_grad[...], mix_near[...])
    part(first_grad, section, True)[...] = contract_last(mixed_grad[...], mix_far[...])
    grad = first_grad[...]
    xhat, scale = nrm_stats(merged[...])
    gain_grad[...] = jnp.sum(grad * xhat, axis=0, keepdims=True)
    bias_grad[...] = jnp.sum(grad, axis=0, keepdims=True)
    gain = vector(section, near_v, far_v, 0, merged.shape[1] // 2)
    total = residual_grad[...] + nrm_back(xhat, scale, grad, gain)
    merged_low[...] = total.astype(LOW)
    merged_t[...] = total.T.astype(LOW)


def unmerge_kernel(where, merged_low, near_w, far_w, input_grad, skip_grad):
    near = contract_last(merged_low[...], near_w[...]).astype(LOW)
    far = contract_last(merged_low[...], far_w[...]).astype(LOW)
    input_grad[...] = jnp.where(where[0] == 0, near, far)
    skip_grad[...] = jnp.where(where[0] == 0, far, near)


def shaped(shape, kind):
    return jax.ShapeDtypeStruct(shape, kind)


def plain_call(kernel, made, operands, grant, scratch=(), scalars=0):
    cost = sum(x.size * x.dtype.itemsize for x in operands)
    specs = [pl.BlockSpec(memory_space=pltpu.SMEM)] * scalars
    specs += [pl.BlockSpec(memory_space=pltpu.VMEM)] * (len(operands) - scalars)
    return pl.pallas_call(
        kernel,
        out_shape=made,
        in_specs=specs,
        out_specs=[pl.BlockSpec(memory_space=pltpu.VMEM)] * len(made),
        scratch_shapes=list(scratch),
        compiler_params=pltpu.CompilerParams(vmem_limit_bytes=grant << 20),
        cost_estimate=pl.CostEstimate(
            flops=128 * cost, bytes_accessed=cost, transcendentals=0
        ),
    )(*operands)


def feed_call(where, pack_near, pack_far, top, residual, near_v, far_v, up_near, up_far, down_near, down_far):
    rows, width = top.shape
    hidden = up_near.shape[1]
    steps = 4
    tile, last = hidden // steps, steps // 2 - 1
    half = width // 2

    def whole(*shape):
        return pl.BlockSpec(shape, lambda j, w: (0,) * len(shape))

    def spot(j, w):
        return (j // (steps // 2) + w[0]) % 2 * (steps // 2) + j % (steps // 2)

    def near(j):
        return jnp.minimum(j, last)

    def far(j):
        return jnp.maximum(j - last - 1, 0)

    in_specs = [
        whole(rows, width), whole(rows, width), whole(rows, width), whole(rows, width),
        whole(*near_v.shape), whole(*far_v.shape),
        pl.BlockSpec((half, tile), lambda j, w: (0, spot(j, w))),
        pl.BlockSpec((half, tile), lambda j, w: (0, spot(j, w))),
        pl.BlockSpec((tile, width), lambda j, w: (near(j), 0)),
        pl.BlockSpec((tile, width), lambda j, w: (far(j), 0)),
    ]
    out_specs = [
        pl.BlockSpec((rows, tile), lambda j, w: (0, near(j))),
        pl.BlockSpec((rows, tile), lambda j, w: (0, far(j))),
        pl.BlockSpec((tile, rows), lambda j, w: (spot(j, w), 0)),
        pl.BlockSpec((1, tile), lambda j, w: (0, spot(j, w))),
        whole(rows, width), whole(rows, width), whole(rows, width), whole(width, rows),
        whole(1, width), whole(1, width),
    ]
    made = [
        shaped((rows, hidden // 2), LOW), shaped((rows, hidden // 2), LOW),
        shaped((hidden, rows), LOW), shaped((1, hidden), FULL),
        shaped((rows, width), LOW), shaped((rows, width), FULL), shaped((rows, width), LOW),
        shaped((width, rows), LOW), shaped((1, width), FULL), shaped((1, width), FULL),
    ]
    weights = 4 * width * hidden
    return pl.pallas_call(
        feed_kernel,
        out_shape=made,
        grid_spec=pltpu.PrefetchScalarGridSpec(
            num_scalar_prefetch=1,
            grid=(steps,),
            in_specs=in_specs,
            out_specs=out_specs,
            scratch_shapes=[pltpu.VMEM((rows, width), FULL)] * 2,
        ),
        compiler_params=pltpu.CompilerParams(
            dimension_semantics=("arbitrary",), vmem_limit_bytes=24 << 20
        ),
        cost_estimate=pl.CostEstimate(
            flops=4 * rows * weights, bytes_accessed=weights, transcendentals=rows * hidden
        ),
        name="feed",
    )(where, pack_near, pack_far, top, residual, near_v, far_v, up_near, up_far, down_near, down_far)


def pick(value, spot, axis=0):
    return lax.dynamic_index_in_dim(value, spot, axis, keepdims=False)


def gather_left(torus, axes, own, far):
    chip = jnp.concatenate([own, far], axis=0)
    lead = torus.order(axes)[0]
    return jnp.concatenate([chip, torus.flip(chip, lead)], axis=0)


def gather_right(torus, axis, own):
    lead, rest = torus.order(axis)
    columns, tokens = own.shape
    split = own.reshape(*(2,) * torus.power, columns // torus.count, tokens)
    place = [torus.power - 1 - bit for bit in (lead, *rest)]
    split = split.transpose(*place, torus.power, torus.power + 1)
    split = split.reshape(2, columns // 2, tokens)
    here = torus.bit(lead)
    near = jnp.stack([pick(split, here), torus.flip(pick(split, 1 - here), lead)])
    far = pair(near)
    return jnp.concatenate([near[0], far[0], near[1], far[1]], axis=1)


def reduce_grad(torus, axis, left, right):
    rest = torus.order(axis)[1]
    halves = right.reshape(2, -1, right.shape[1])
    here = torus.bit(rest[0])
    sent = dot(pick(halves, 1 - here), left).astype(LOW)
    sent = torus.flip(sent, rest[0])
    total = dot(pick(halves, here), left) + sent.astype(FULL)
    for bit in rest[1:]:
        here = torus.bit(bit)
        held = total.astype(LOW).reshape(2, -1, left.shape[1])
        sent = torus.flip(pick(held, 1 - here), bit)
        total = pick(held, here).astype(FULL) + sent.astype(FULL)
    return total


def body(
    layer_input,
    skip_input,
    segment_ids,
    out_cotangent,
    merger,
    mixing,
    readout,
    expand,
    narrow,
    first_gain,
    first_bias,
    second_gain,
    second_bias,
    up_bias,
):
    torus = Torus(lax.axis_size("dp"))
    section = lax.axis_index("section")
    rows, width = layer_input.shape
    first_core = section == 0

    def packed(parts):
        bounds, total = [], 0
        for item in parts:
            bounds.append((total, total + item.shape[0]))
            total += item.shape[0]
        placed = [jnp.pad(item, (low, total - high)) for item, (low, high) in zip(parts, bounds)]
        return sum(placed[1:], placed[0]), bounds

    def mine(value):
        half = value.shape[-1] // 2
        return lax.dynamic_slice_in_dim(value, section * half, half, value.ndim - 1)

    merger_far = pair(merger)
    near_v, _ = packed((first_gain, first_bias, second_gain, second_bias, up_bias))
    near_v = near_v[None]
    far_v = pair(near_v)
    mixing_far = pair(mixing)
    readout_far = pair(readout)
    expand_far = pair(expand)
    narrow_far = pair(narrow)
    top_low = pair(out_cotangent)

    where = section.astype(jnp.int32).reshape(1)
    frames_mine = jnp.where(first_core, layer_input, skip_input)
    frames_other = jnp.where(first_core, skip_input, layer_input)
    segments = pick(segment_ids[0], section)[None]
    flat, tall, thin = (rows, width), (width, rows), (rows, width // 2)
    line = shaped((1, width), FULL)

    merged, low_near, low_far, top_t = plain_call(
        merge_kernel,
        [shaped(flat, FULL), shaped(thin, LOW), shaped(thin, LOW), shaped(tall, LOW)],
        (where, layer_input, skip_input, merger, merger_far, near_v, far_v, top_low), 56, scalars=1,
    )
    mixed, pack_near, pack_far, residual = plain_call(
        attend_kernel,
        [shaped((rows, 3 * width), LOW), shaped(flat, LOW), shaped(flat, LOW), shaped(flat, FULL)],
        (where, low_near, low_far, merged, segments, mixing, mixing_far, readout, readout_far,
         near_v, far_v),
        24, scratch=[pltpu.VMEM(flat, LOW)], scalars=1,
    )
    (act_near, act_far, lifted_t, up_bias_grad, output, residual_grad, residual_low, residual_t,
     second_gain_grad, second_bias_grad) = feed_call(
        where, pack_near, pack_far, top_low, residual, near_v, far_v, expand, expand_far, narrow,
        narrow_far,
    )
    block_output = pair(output)
    mixed_grad, mixed_t = plain_call(
        unattend_kernel,
        [shaped((rows, 3 * width), LOW), shaped((3 * width, rows), LOW)],
        (where, mixed, residual_low, segments, readout, readout_far),
        16, scratch=[pltpu.VMEM(flat, LOW)], scalars=1,
    )
    merged_low, merged_t, first_gain_grad, first_bias_grad = plain_call(
        unmix_kernel, [shaped(flat, LOW), shaped(tall, LOW), line, line],
        (where, mixed_grad, mixing, mixing_far, merged, residual_grad, near_v, far_v),
        16, scratch=[pltpu.VMEM(flat, FULL)], scalars=1,
    )
    input_grad, skip_grad = plain_call(
        unmerge_kernel, [shaped(flat, LOW)] * 2,
        (where, merged_low, merger, merger_far), 12, scalars=1,
    )

    def left_of(axes, near, far):
        return gather_left(torus, axes, near, pair(far))

    def grad_of(axes, left, right_t):
        return reduce_grad(torus, axes, left, gather_right(torus, axes, right_t))

    half = width // 2
    merger_left = left_of("yxyz", frames_mine, frames_other)
    mixing_left = left_of("Zxyz", low_near, low_far)
    mid_left = left_of("zxzy", pack_near, pack_far)
    narrow_left = left_of("xyxz", act_near, act_far)
    narrow_grad = grad_of("xyxz", narrow_left, top_t)
    expand_grad = grad_of("zxzy", mid_left[:, half:], lifted_t)
    readout_grad = grad_of("zyzx", mid_left[:, :half], residual_t)
    mixing_grad = grad_of("Zxyz", mixing_left, mixed_t)
    merger_grad = grad_of("yxyz", merger_left, merged_t)

    small, bounds = packed(
        [
            item[0]
            for item in (
                first_gain_grad, first_bias_grad, second_gain_grad, second_bias_grad, up_bias_grad
            )
        ]
    )
    small = small.reshape(-1, 128)
    small = small + pair(small)
    for bit in torus.bits["z"] + torus.bits["y"] + torus.bits["x"]:
        small = small + torus.flip(small, bit)
    small = small.reshape(-1)
    expand_out = expand_grad.T
    matrices = (merger_grad.T, mixing_grad.T, readout_grad.T, expand_out, narrow_grad.T)
    return (block_output, input_grad, skip_grad) + matrices + tuple(
        mine(small[low:high]) for low, high in bounds
    )


def solution(mesh):
    tokens = P(("section", "dp"), None)
    matrix, vector = P("section", None), P("section")
    placed = (tokens, tokens, P("dp", None, None), tokens) + (matrix,) * 5 + (vector,) * 5
    made = (tokens,) * 3 + (P("section", "dp"),) * 5 + (vector,) * 5
    return jax.shard_map(body, mesh=mesh, in_specs=placed, out_specs=made, check_vma=False)
```
